1024 devices in a mesh: outer: 8 (over x, core), inner: 128 (over z, y).
Axes of the slice: x: 4, y: 8, z: 16, core: 2. Of those that a mesh axis runs over, the one named last changes fastest.
Arguments:
- leaf_q: float32 [262144, 128], P(('outer', 'inner')), may hold values from -0.375 to 0.375
- q_cot: float32 [262144, 128], P(('outer', 'inner')), may hold values from -6 to 6
- leaf_tri: float32 [131072, 128], P(('outer', 'inner')), as said below
- node_blocks: bfloat16 [5, 131072, 128], P(None, ('outer', 'inner')), as said below
- node_tri: bfloat16 [5, 131072, 128], P(None, ('outer', 'inner')), as said below
- root_cot: float32 [128, 128], replicated, may hold values from -6 to 6
Outputs:
- mat_grad: float32 [262144, 128], P(('outer', 'inner'))
The draws below stay inside these ranges and needn't reach their ends.
Inputs may be any that keep to these rules, and one draw needn't show every extreme that they name: `leaf_tri`: upper triangular; diagonal between 1 and 3. `node_blocks`: at each level, every leaf holds the block of its own child subtree, and all leaves of one child subtree hold equal blocks. `node_tri`: upper triangular with diagonal between 1 and 3; at each level all leaves of one node hold equal triangles.
All inputs are finite; a program needn't handle non-finite values.
Results may differ from the reference program's by a relative error of at most 0.0003.
Values sent between devices are 32-bit elements; how exact they have to be, the bound alone decides.
No kernel may reach another device: no remote copies, remote signals or barrier semaphores. Data moves between devices by JAX's collectives and lax.ppermute only.
A program may use at most 32 MiB of HBM per device.

```python
import math
import jax
import jax.numpy as jnp
from jax import lax

N = 128
BLOCK = 32
ROWS_DEV = 256
ROWS = 262144
N_OUTER = 8
N_INNER = 128
DEVICES = 1024


def fan_list_drawn():
    fanins = []
    remain = N_INNER
    while remain > 1:
        factor = min(remain, 4)
        fanins.append(factor)
        remain = remain // factor
    fanins.append(N_OUTER)
    return fanins


def upper_triangle(key, matrix_count):
    diag_key, off_key = jax.random.split(key)
    diagonal = jnp.exp(jax.random.uniform(diag_key, (matrix_count, N), minval=0.0, maxval=math.log(3.0)))
    above = jax.random.normal(off_key, (matrix_count, N, N)) * (0.7 * N ** (-0.5))
    return jnp.triu(above, 1) + diagonal[:, :, None] * jnp.eye(N, dtype=jnp.float32)


def draw_leaf_tri(key, part):
    return upper_triangle(jax.random.fold_in(key, 11), DEVICES).reshape(DEVICES * N, N)


def draw_node_blocks(key, part):
    fanins = fan_list_drawn()
    pieces = []
    stride = 1
    for height in range(len(fanins)):
        block_key = jax.random.fold_in(jax.random.fold_in(key, 23), height)
        shape_here = (DEVICES // stride, N, N)
        matrices = jax.random.normal(block_key, shape_here) * (2.0 * N) ** (-0.5)
        pieces.append(jnp.repeat(matrices, stride, axis=0))
        stride = stride * fanins[height]
    return jnp.stack(pieces).reshape(len(fanins), DEVICES * N, N).astype(jnp.bfloat16)


def draw_node_tri(key, part):
    fanins = fan_list_drawn()
    pieces = []
    stride = 1
    for height in range(len(fanins)):
        node_stride = stride * fanins[height]
        tri_key = jax.random.fold_in(jax.random.fold_in(key, 37), height)
        matrices = upper_triangle(tri_key, DEVICES // node_stride)
        pieces.append(jnp.repeat(matrices, node_stride, axis=0))
        stride = node_stride
    return jnp.stack(pieces).reshape(len(fanins), DEVICES * N, N).astype(jnp.bfloat16)


def block_scale(key, shape, shards, smallest, high):
    def one(position, parts):
        steps = jax.random.uniform(jax.random.fold_in(jax.random.fold_in(key, 6), position), (parts,), jnp.float32, smallest / len(shards), high / len(shards))
        return jnp.repeat(jnp.exp(steps), shape[position] // parts).reshape((-1,) + (1,) * (len(shape) - position - 1))

    factor_of = one(*shards[0])
    for cut in shards[1:]:
        factor_of = factor_of * one(*cut)
    return factor_of


def noise(rng, shape, width, bound, cuts=(), kind=jnp.bfloat16):
    drawn = width * jax.random.normal(rng, shape, jnp.float32)
    if cuts:
        drawn = drawn * block_scale(rng, shape, cuts, -0.22, 0.18)
    return jnp.clip(drawn, -bound, bound).astype(kind)


def setup_inputs(seed: int = 0) -> dict:
    splits = jax.random.split(jax.random.key(seed), 7)
    return {
        "leaf_q": noise(splits[0], (ROWS, N), ROWS_DEV ** -0.5, 0.375, ((0, 1024),), jnp.float32),
        "q_cot": noise(splits[1], (ROWS, N), 1.0, 6.0, ((0, 1024),), jnp.float32),
        "leaf_tri": draw_leaf_tri(jax.random.fold_in(splits[6], 71), 0),
        "node_blocks": draw_node_blocks(jax.random.fold_in(splits[6], 71), 0),
        "node_tri": draw_node_tri(jax.random.fold_in(splits[6], 71), 0),
        "root_cot": noise(splits[5], (N, N), 1.0, 6.0, (), jnp.float32),
    }


def fan_list():
    fanins = []
    remain = N_INNER
    while remain > 1:
        factor = min(remain, 4)
        fanins.append(factor)
        remain = remain // factor
    fanins.append(N_OUTER)
    return fanins


def matmul(left_side, right_side):
    return jnp.matmul(left_side, right_side, precision=lax.Precision.HIGHEST)


def flip_last(matrix):
    return jnp.swapaxes(matrix, -1, -2)


def mirror_lower(matrix):
    return jnp.tril(matrix) + flip_last(jnp.tril(matrix, -1))


def small_inverse(block):
    order = block.shape[-1]
    diag_vals = jnp.diagonal(block, axis1=-2, axis2=-1)
    eye_small = jnp.eye(order, dtype=jnp.float32)
    nilpotent = -jnp.triu(block, 1) / diag_vals[..., :, None]
    product = eye_small + nilpotent
    power = 2
    while power < order:
        nilpotent = matmul(nilpotent, nilpotent)
        product = matmul(product, eye_small + nilpotent)
        power = power * 2
    return product / diag_vals[..., None, :]


def tri_inverse(triangle):
    order = triangle.shape[-1]
    count = order // BLOCK
    inverses = [small_inverse(triangle[..., k * BLOCK:(k + 1) * BLOCK, k * BLOCK:(k + 1) * BLOCK]) for k in range(count)]
    span = BLOCK
    while len(inverses) > 1:
        joined = []
        for pair in range(len(inverses) // 2):
            start = pair * 2 * span
            upper_inv = inverses[2 * pair]
            lower_inv = inverses[2 * pair + 1]
            corner = triangle[..., start:start + span, start + span:start + 2 * span]
            linked = -matmul(matmul(upper_inv, corner), lower_inv)
            top_rows = jnp.concatenate([upper_inv, linked], axis=-1)
            bottom_rows = jnp.concatenate([jnp.zeros_like(lower_inv), lower_inv], axis=-1)
            joined.append(jnp.concatenate([top_rows, bottom_rows], axis=-2))
        inverses = joined
        span = span * 2
    return inverses[0]


def right_solve(triangle, values):
    return matmul(values, flip_last(tri_inverse(triangle)))


def reference(leaf_q, q_cot, leaf_tri, node_blocks, node_tri, root_cot):
    fanins = fan_list()
    levels_count = len(fanins)
    blocks_all = node_blocks.astype(jnp.float32).reshape(levels_count, DEVICES, N, N)
    tris_all = node_tri.astype(jnp.float32).reshape(levels_count, DEVICES, N, N)
    leaf_rows = leaf_q.reshape(DEVICES, ROWS_DEV, N)
    cot_rows = q_cot.reshape(DEVICES, ROWS_DEV, N)
    leaf_tris = leaf_tri.reshape(DEVICES, N, N)
    leaf_sums = matmul(flip_last(leaf_rows), cot_rows)
    child_sums = [leaf_sums]
    strides = []
    stride = 1
    for height in range(levels_count):
        factor = fanins[height]
        strides.append(stride)
        child_blocks = blocks_all[height, ::stride]
        projected = matmul(flip_last(child_blocks), child_sums[-1])
        child_sums.append(jnp.sum(projected.reshape(-1, factor, N, N), axis=1))
        stride = stride * factor
    upper_path = None
    cot_tri = root_cot[None]
    for height in reversed(range(levels_count)):
        factor = fanins[height]
        stride = strides[height]
        child_blocks = blocks_all[height, ::stride]
        node_tris = tris_all[height, ::stride * factor]
        node_sums = child_sums[height + 1]
        own_sums = child_sums[height]
        if upper_path is None:
            middle = matmul(node_tris, flip_last(cot_tri)) - flip_last(node_sums)
            spread = jnp.repeat(mirror_lower(middle), factor, axis=0)
            right_side = own_sums + matmul(child_blocks, spread)
            upper_path = child_blocks
        else:
            middle = matmul(node_tris, flip_last(cot_tri)) - matmul(upper_path, flip_last(node_sums))
            spread = jnp.repeat(mirror_lower(middle), factor, axis=0)
            path_copies = jnp.repeat(upper_path, factor, axis=0)
            right_side = matmul(own_sums, flip_last(path_copies)) + matmul(child_blocks, spread)
            upper_path = matmul(child_blocks, path_copies)
        node_inverse = jnp.repeat(tri_inverse(node_tris), factor, axis=0)
        cot_tri = matmul(right_side, flip_last(node_inverse))
    leaf_cot = matmul(cot_rows, flip_last(upper_path))
    middle = matmul(leaf_tris, flip_last(cot_tri)) - matmul(upper_path, flip_last(leaf_sums))
    gradient = right_solve(leaf_tris, leaf_cot + matmul(leaf_rows, mirror_lower(middle)))
    return gradient.reshape(DEVICES * ROWS_DEV, N)
```

```python
import jax
import jax.numpy as jnp
from jax import lax
from jax.experimental import pallas as pl
from jax.experimental.pallas import tpu as pltpu
from jax.sharding import Mesh, PartitionSpec as P

N = 128
BLOCK = 32
PIECE = 16
ROWS = 256
LEVELS = 5
N_Y = 8
N_Z = 16
N_OUTER = 8

F32 = jnp.float32
BF16 = jnp.bfloat16


def split3(value):
    high = value.astype(BF16)
    rest = value - high.astype(F32)
    middle = rest.astype(BF16)
    low = (rest - middle.astype(F32)).astype(BF16)
    return high, middle, low


def dot(left, right, dims):
    return lax.dot_general(left, right, (dims, ((), ())), preferred_element_type=F32)


NN = ((1,), (0,))
NT = ((1,), (1,))


def mm(left, right, dims=NN):
    rows = left.shape[0]
    lh, lm, ll = split3(left)
    rh, rm, rl = split3(right)
    first = dot(jnp.concatenate([lh, lm, ll], axis=0), rh, dims)
    second = dot(jnp.concatenate([lh, lm], axis=0), rm, dims)
    third = dot(lh, rl, dims)
    small = first[2 * rows :] + second[rows:] + third
    return first[:rows] + (first[rows : 2 * rows] + second[:rows] + small)


def mm_exact(left, right, dims=NN):
    rows = left.shape[0]
    lh, lm, ll = split3(left)
    full = dot(jnp.concatenate([lh, lm, ll], axis=0), right, dims)
    return full[:rows] + (full[rows : 2 * rows] + full[2 * rows :])


def iotas(rows=N):
    return (
        lax.broadcasted_iota(jnp.int32, (rows, N), 0),
        lax.broadcasted_iota(jnp.int32, (rows, N), 1),
    )


def mirror_lower(matrix):
    row, col = iotas()
    return jnp.where(row >= col, matrix, matrix.T)


def tri_inverse(triangle):
    row, col = iotas()
    on_diag = row == col
    diag_col = jnp.sum(jnp.where(on_diag, triangle, 0.0), axis=1, keepdims=True)
    diag_row = jnp.sum(jnp.where(on_diag, triangle, 0.0), axis=0, keepdims=True)
    same = (row // BLOCK) == (col // BLOCK)
    strict = jnp.where(same & (row < col), -triangle, 0.0) / diag_col

    def packed(matrix):
        return (matrix[0:32] + matrix[32:64]) + (matrix[64:96] + matrix[96:128])

    def spread(rows):
        return jnp.where(same, jnp.concatenate([rows] * 4, axis=0), 0.0)

    small_row, small_col = iotas(BLOCK)
    eye = jnp.where(small_row == small_col % BLOCK, 1.0, 0.0).astype(F32)
    power = packed(strict)
    product = eye + power
    power = mm(power, strict)
    for _ in range(3):
        both = mm(jnp.concatenate([power, product], axis=0), spread(power))
        product = product + both[BLOCK:]
        power = both[:BLOCK]
    product = product + mm(product, spread(power))
    inverse = product / diag_row
    block_inverse = spread(inverse)
    corner = jnp.where((row // 64 == col // 64) & (row // 32 < col // 32), triangle, 0.0)
    linked = mm(mm(inverse, corner), block_inverse)
    odd = (small_col // BLOCK) % 2 == 1
    top = jnp.where(odd, -linked, inverse)
    bottom = jnp.where(odd, inverse, 0.0)
    pair = jnp.concatenate([top, bottom], axis=0)
    pair_inverse = jnp.where(row // 64 == col // 64, jnp.concatenate([pair, pair], axis=0), 0.0)
    corner = jnp.where(row // 64 < col // 64, triangle, 0.0)
    linked = mm(mm(pair, corner), pair_inverse)
    upper = pair_inverse[:64] - linked
    return jnp.concatenate([upper, pair_inverse[64:]], axis=0)


def leaf_values(leaf_q, q_cot, block_1, block_2):
    sums_t = mm(q_cot.T, leaf_q)
    first_t = mm_exact(sums_t, block_1)
    second_t = mm_exact(first_t, block_2)
    return sums_t, first_t, second_t


def leaf_kernel(q_ref, g_ref, blocks_ref, sums_ref, send_ref):
    sums_t, first_t, second_t = leaf_values(q_ref[...], g_ref[...], blocks_ref[0], blocks_ref[1])
    sums_ref[...] = sums_t
    for y in range(N_Y):
        send_ref[y, 0:PIECE] = first_t[y * PIECE : (y + 1) * PIECE]
        send_ref[y, PIECE : 2 * PIECE] = second_t[y * PIECE : (y + 1) * PIECE]


def near_kernel(z_ref, recv_ref, blocks_ref, kept_ref, send_ref):
    z = z_ref[0]
    halves = [sum(recv_ref[4 * h + k, 0:PIECE] for k in range(4)) for h in range(2)]
    kept_ref[0] = halves[0]
    kept_ref[1] = halves[1]
    second = sum(recv_ref[k, PIECE : 2 * PIECE] for k in range(N_Y))
    third = mm_exact(second, blocks_ref[2])
    fourth = mm_exact(third, blocks_ref[3])
    for peer in range(N_Z):
        same_pair = (z // 2) == (peer // 2)
        same_octet = (z // 8) == (peer // 8)
        send_ref[peer] = jnp.where(same_pair, second, jnp.where(same_octet, third, fourth))


def far_kernel(z_ref, recv_ref, blocks_ref, kept_ref, send_ref):
    z = z_ref[0]
    zero = jnp.zeros((PIECE, N), F32)
    second, third, fourth = zero, zero, zero
    for peer in range(N_Z):
        same_pair = (z // 2) == (peer // 2)
        same_octet = (z // 8) == (peer // 8)
        value = recv_ref[peer]
        second = second + jnp.where(same_pair, value, zero)
        third = third + jnp.where(same_octet & jnp.logical_not(same_pair), value, zero)
        fourth = fourth + jnp.where(same_octet, zero, value)
    third = third + mm_exact(second, blocks_ref[2])
    fourth = fourth + mm_exact(third, blocks_ref[3])
    fifth = mm_exact(fourth, blocks_ref[4])
    kept_ref[0] = second
    kept_ref[1] = third
    kept_ref[2] = fourth
    for peer in range(N_OUTER):
        send_ref[peer] = fifth


def join_kernel(recv_ref, halves_ref, kept_ref, send_ref):
    fifth = sum(recv_ref[k] for k in range(N_OUTER))
    for y in range(N_Y):
        send_ref[y, 0:PIECE] = halves_ref[y // 4]
        for level in range(3):
            send_ref[y, (level + 1) * PIECE : (level + 2) * PIECE] = kept_ref[level]
        send_ref[y, 4 * PIECE : 5 * PIECE] = fifth


def prepare_kernel(tri_ref, g_ref, blocks_ref, tris_ref, root_ref, link_ref, gain_ref, inverse_ref, base_ref, top_ref):
    leaf = tri_ref[...]
    tris = [leaf] + [tris_ref[level].astype(F32) for level in range(LEVELS)]
    inverses = [tri_inverse(tri) for tri in tris]
    paths = [None] * (LEVELS + 1)
    paths[LEVELS - 1] = blocks_ref[LEVELS - 1].astype(F32)
    for level in reversed(range(LEVELS - 1)):
        paths[level] = mm(blocks_ref[level].astype(F32), paths[level + 1])
    for level in reversed(range(LEVELS)):
        link = mm(tris[level], inverses[level + 1])
        link_ref[level] = link
        if level == LEVELS - 1:
            gain_ref[level] = link - paths[level]
        else:
            gain_ref[level] = mm(link, paths[level + 1]) - paths[level]
    inverse_ref[...] = inverses[0]
    base_ref[...] = mm(g_ref[...], mm(inverses[0], paths[0]), NT)
    top_ref[...] = mm(tris[LEVELS], root_ref[...], NT)


def descend_kernel(recv_ref, sums_ref, q_ref, blocks_ref, link_ref, gain_ref, inverse_ref, base_ref, top_ref, out_ref):
    def gathered(level):
        return jnp.concatenate(
            [recv_ref[y, (level - 1) * PIECE : level * PIECE] for y in range(N_Y)], axis=0
        )

    middle = top_ref[...] - gathered(LEVELS)
    for level in reversed(range(LEVELS)):
        own = gathered(level) if level else sums_ref[...]
        spread = mm(link_ref[level], mirror_lower(middle))
        middle = mm(gain_ref[level], own) + mm_exact(spread, blocks_ref[level], NT)
    inner = mm(q_ref[...], mirror_lower(middle))
    out_ref[...] = base_ref[...] + mm(inner, inverse_ref[...], NT)


def f32(*shape):
    return jax.ShapeDtypeStruct(shape, F32)


SMEM = pl.BlockSpec(memory_space=pltpu.SMEM)
VMEM = pl.BlockSpec(memory_space=pltpu.VMEM)


def on_device(leaf_q, q_cot, leaf_tri, node_blocks, node_tri, root_cot):
    z = lax.axis_index("z").astype(jnp.int32).reshape(1)
    sums, send = pl.pallas_call(
        leaf_kernel, out_shape=(f32(N, N), f32(N_Y, 2 * PIECE, N)), name="leaf"
    )(leaf_q, q_cot, node_blocks)
    recv = lax.all_to_all(send, "y", 0, 0)
    halves, send = pl.pallas_call(
        near_kernel,
        in_specs=[SMEM, VMEM, VMEM],
        out_shape=(f32(2, PIECE, N), f32(N_Z, PIECE, N)),
        name="near",
    )(z, recv, node_blocks)
    recv = lax.all_to_all(send, "z", 0, 0)
    kept, send = pl.pallas_call(
        far_kernel,
        in_specs=[SMEM, VMEM, VMEM],
        out_shape=(f32(3, PIECE, N), f32(N_OUTER, PIECE, N)),
        name="far",
    )(z, recv, node_blocks)
    recv = lax.all_to_all(send, "outer", 0, 0)
    send = pl.pallas_call(join_kernel, out_shape=f32(N_Y, 5 * PIECE, N), name="join")(recv, halves, kept)
    recv = lax.all_to_all(send, "y", 0, 0)
    link, gain, inverse, base, top = pl.pallas_call(
        prepare_kernel,
        out_shape=(f32(LEVELS, N, N), f32(LEVELS, N, N), f32(N, N), f32(ROWS, N), f32(N, N)),
        name="prepare",
    )(leaf_tri, q_cot, node_blocks, node_tri, root_cot)
    return pl.pallas_call(descend_kernel, out_shape=f32(ROWS, N), name="descend")(
        recv, sums, leaf_q, node_blocks, link, gain, inverse, base, top
    )


def solution(mesh):
    split = Mesh(mesh.devices.reshape(N_OUTER, N_Z, N_Y), ("outer", "z", "y"))
    every = ("outer", "z", "y")
    return jax.shard_map(
        on_device,
        mesh=split,
        in_specs=(
            P(every, None),
            P(every, None),
            P(every, None),
            P(None, every, None),
            P(None, every, None),
            P(),
        ),
        out_specs=P(every, None),
        check_vma=False,
    )
```

```python
import jax
import jax.numpy as jnp
from jax import lax
from jax.experimental import pallas as pl
from jax.experimental.pallas import tpu as pltpu
from jax.sharding import Mesh, PartitionSpec as P

N = 128
BLOCK = 32
PIECE = 16
ROWS = 256
LEVELS = 5
N_Y = 8
N_Z = 16
N_OUTER = 8

F32 = jnp.float32
BF16 = jnp.bfloat16


def split3(value):
    high = value.astype(BF16)
    rest = value - high.astype(F32)
    middle = rest.astype(BF16)
    low = (rest - middle.astype(F32)).astype(BF16)
    return high, middle, low


def dot(left, right, dims):
    return lax.dot_general(left, right, (dims, ((), ())), preferred_element_type=F32)


NN = ((1,), (0,))
NT = ((1,), (1,))


def mm(left, right, dims=NN):
    rows = left.shape[0]
    lh, lm, ll = split3(left)
    rh, rm, rl = split3(right)
    first = dot(jnp.concatenate([lh, lm, ll], axis=0), rh, dims)
    second = dot(jnp.concatenate([lh, lm], axis=0), rm, dims)
    third = dot(lh, rl, dims)
    small = first[2 * rows :] + second[rows:] + third
    return first[:rows] + (first[rows : 2 * rows] + second[:rows] + small)


def mm_exact(left, right, dims=NN):
    rows = left.shape[0]
    lh, lm, ll = split3(left)
    full = dot(jnp.concatenate([lh, lm, ll], axis=0), right, dims)
    return full[:rows] + (full[rows : 2 * rows] + full[2 * rows :])


def iotas(rows=N):
    return (
        lax.broadcasted_iota(jnp.int32, (rows, N), 0),
        lax.broadcasted_iota(jnp.int32, (rows, N), 1),
    )


def mirror_lower(matrix):
    row, col = iotas()
    return jnp.where(row >= col, matrix, matrix.T)


def tri_inverse(triangle):
    row, col = iotas()
    on_diag = row == col
    diag_col = jnp.sum(jnp.where(on_diag, triangle, 0.0), axis=1, keepdims=True)
    diag_row = jnp.sum(jnp.where(on_diag, triangle, 0.0), axis=0, keepdims=True)
    same = (row // BLOCK) == (col // BLOCK)
    strict = jnp.where(same & (row < col), -triangle, 0.0) / diag_col

    def packed(matrix):
        return (matrix[0:32] + matrix[32:64]) + (matrix[64:96] + matrix[96:128])

    def spread(rows):
        return jnp.where(same, jnp.concatenate([rows] * 4, axis=0), 0.0)

    small_row, small_col = iotas(BLOCK)
    eye = jnp.where(small_row == small_col % BLOCK, 1.0, 0.0).astype(F32)
    power = packed(strict)
    product = eye + power
    power = mm(power, strict)
    for _ in range(3):
        both = mm(jnp.concatenate([power, product], axis=0), spread(power))
        product = product + both[BLOCK:]
        power = both[:BLOCK]
    product = product + mm(product, spread(power))
    inverse = product / diag_row
    block_inverse = spread(inverse)
    corner = jnp.where((row // 64 == col // 64) & (row // 32 < col // 32), triangle, 0.0)
    linked = mm(mm(inverse, corner), block_inverse)
    odd = (small_col // BLOCK) % 2 == 1
    top = jnp.where(odd, -linked, inverse)
    bottom = jnp.where(odd, inverse, 0.0)
    pair = jnp.concatenate([top, bottom], axis=0)
    pair_inverse = jnp.where(row // 64 == col // 64, jnp.concatenate([pair, pair], axis=0), 0.0)
    corner = jnp.where(row // 64 < col // 64, triangle, 0.0)
    linked = mm(mm(pair, corner), pair_inverse)
    upper = pair_inverse[:64] - linked
    return jnp.concatenate([upper, pair_inverse[64:]], axis=0)


def leaf_kernel(q_hbm, g_hbm, blocks_hbm, sums_ref, send_ref, q_ref, g_ref, blocks_ref, sems):
    copies = [
        pltpu.make_async_copy(g_hbm, g_ref, sems.at[0]),
        pltpu.make_async_copy(q_hbm, q_ref, sems.at[1]),
        pltpu.make_async_copy(blocks_hbm.at[0:2], blocks_ref, sems.at[2]),
    ]
    for copy in copies:
        copy.start()
    copies[0].wait()
    copies[1].wait()
    sums_t = mm(g_ref[...].T, q_ref[...])
    sums_ref[...] = sums_t
    copies[2].wait()
    first_t = mm_exact(sums_t, blocks_ref[0])
    second_t = mm_exact(first_t, blocks_ref[1])
    for y in range(N_Y):
        send_ref[y, 0:PIECE] = first_t[y * PIECE : (y + 1) * PIECE]
        send_ref[y, PIECE : 2 * PIECE] = second_t[y * PIECE : (y + 1) * PIECE]


def near_kernel(z_ref, recv_ref, blocks_ref, kept_ref, send_ref):
    z = z_ref[0]
    halves = [sum(recv_ref[4 * h + k, 0:PIECE] for k in range(4)) for h in range(2)]
    kept_ref[0] = halves[0]
    kept_ref[1] = halves[1]
    second = sum(recv_ref[k, PIECE : 2 * PIECE] for k in range(N_Y))
    third = mm_exact(second, blocks_ref[2])
    fourth = mm_exact(third, blocks_ref[3])
    for peer in range(N_Z):
        same_pair = (z // 2) == (peer // 2)
        same_octet = (z // 8) == (peer // 8)
        send_ref[peer] = jnp.where(same_pair, second, jnp.where(same_octet, third, fourth))


def far_kernel(z_ref, recv_ref, blocks_ref, after_ref, kept_ref, send_ref):
    z = z_ref[0]
    zero = jnp.zeros((PIECE, N), F32)
    second, third, fourth = zero, zero, zero
    for peer in range(N_Z):
        same_pair = (z // 2) == (peer // 2)
        same_octet = (z // 8) == (peer // 8)
        value = recv_ref[peer]
        second = second + jnp.where(same_pair, value, zero)
        third = third + jnp.where(same_octet & jnp.logical_not(same_pair), value, zero)
        fourth = fourth + jnp.where(same_octet, zero, value)
    third = third + mm_exact(second, blocks_ref[2])
    fourth = fourth + mm_exact(third, blocks_ref[3])
    fifth = mm_exact(fourth, blocks_ref[4])
    kept_ref[0] = second
    kept_ref[1] = third
    kept_ref[2] = fourth
    for peer in range(N_OUTER):
        send_ref[peer] = fifth


def join_kernel(recv_ref, halves_ref, kept_ref, after_ref, send_ref):
    fifth = sum(recv_ref[k] for k in range(N_OUTER))
    for y in range(N_Y):
        send_ref[y, 0:PIECE] = halves_ref[y // 4]
        for level in range(3):
            send_ref[y, (level + 1) * PIECE : (level + 2) * PIECE] = kept_ref[level]
        send_ref[y, 4 * PIECE : 5 * PIECE] = fifth


def inverse_kernel(tri_ref, tris_ref, after_ref, out_ref):
    tris = [tri_ref[...]] + [tris_ref[level].astype(F32) for level in range(LEVELS)]
    for level, tri in enumerate(tris):
        out_ref[level] = tri_inverse(tri)


def chain_kernel(tri_ref, g_ref, blocks_ref, tris_ref, root_ref, inverse_ref, after_ref, link_ref, gain_ref, base_ref, top_ref):
    tris = [tri_ref[...]] + [tris_ref[level].astype(F32) for level in range(LEVELS)]
    paths = [None] * (LEVELS + 1)
    paths[LEVELS - 1] = blocks_ref[LEVELS - 1].astype(F32)
    for level in reversed(range(LEVELS - 1)):
        paths[level] = mm(blocks_ref[level].astype(F32), paths[level + 1])
    for level in reversed(range(LEVELS)):
        link = mm(tris[level], inverse_ref[level + 1])
        link_ref[level] = link
        if level == LEVELS - 1:
            gain_ref[level] = link - paths[level]
        else:
            gain_ref[level] = mm(link, paths[level + 1]) - paths[level]
    base_ref[...] = mm(g_ref[...], mm(inverse_ref[0], paths[0]), NT)
    top_ref[...] = mm(tris[LEVELS], root_ref[...], NT)


def descend_kernel(recv_ref, sums_ref, q_ref, blocks_ref, link_ref, gain_ref, inverse_ref, base_ref, top_ref, out_ref):
    def gathered(level):
        return jnp.concatenate(
            [recv_ref[y, (level - 1) * PIECE : level * PIECE] for y in range(N_Y)], axis=0
        )

    middle = top_ref[...] - gathered(LEVELS)
    for level in reversed(range(LEVELS)):
        own = gathered(level) if level else sums_ref[...]
        spread = mm(link_ref[level], mirror_lower(middle))
        middle = mm(gain_ref[level], own) + mm_exact(spread, blocks_ref[level], NT)
    inner = mm(q_ref[...], mirror_lower(middle))
    out_ref[...] = base_ref[...] + mm(inner, inverse_ref[0], NT)


def kept(*shape):
    return pltpu.VMEM(shape, F32)


def near(value):
    return pltpu.with_memory_space_constraint(value, pltpu.VMEM)


SMEM = pl.BlockSpec(memory_space=pltpu.SMEM)
VMEM = pl.BlockSpec(memory_space=pltpu.VMEM)
PLAIN = pl.BlockSpec(memory_space=pltpu.HBM)


def call(kernel, outs, specs, name, scratch=()):
    return pl.pallas_call(
        kernel,
        in_specs=specs,
        out_shape=outs,
        out_specs=jax.tree.map(lambda _: VMEM, outs),
        scratch_shapes=scratch,
        name=name,
        compiler_params=pltpu.CompilerParams(vmem_limit_bytes=16 << 20),
    )


def on_device(leaf_q, q_cot, leaf_tri, node_blocks, node_tri, root_cot):
    z = lax.axis_index("z").astype(jnp.int32).reshape(1)
    blocks, tris = near(node_blocks), near(node_tri)
    tri, cot, root, rows = near(leaf_tri), near(q_cot), near(root_cot), near(leaf_q)
    scratch = (
        kept(ROWS, N),
        kept(ROWS, N),
        pltpu.VMEM((2, N, N), BF16),
        pltpu.SemaphoreType.DMA((3,)),
    )
    sums, send = call(
        leaf_kernel, (kept(N, N), kept(N_Y, 2 * PIECE, N)), [PLAIN] * 3, "leaf", scratch
    )(leaf_q, q_cot, node_blocks)
    recv = near(lax.all_to_all(send, "y", 0, 0))
    halves, send = call(near_kernel, (kept(2, PIECE, N), kept(N_Z, PIECE, N)), [SMEM, VMEM, VMEM], "near")(
        z, recv, blocks
    )
    halves = near(halves)
    inverses = call(inverse_kernel, kept(LEVELS + 1, N, N), [VMEM] * 3, "inverse")(tri, tris, halves)
    inverses = near(inverses)
    recv = near(lax.all_to_all(send, "z", 0, 0))
    mine, send = call(
        far_kernel, (kept(3, PIECE, N), kept(N_OUTER, PIECE, N)), [SMEM] + [VMEM] * 3, "far"
    )(z, recv, blocks, inverses)
    mine = near(mine)
    link, gain, base, top = call(
        chain_kernel, (kept(LEVELS, N, N), kept(LEVELS, N, N), kept(ROWS, N), kept(N, N)), [VMEM] * 7, "chain"
    )(tri, cot, blocks, tris, root, inverses, mine)
    link, gain, base, top = near(link), near(gain), near(base), near(top)
    recv = near(lax.all_to_all(send, "outer", 0, 0))
    send = call(join_kernel, kept(N_Y, 5 * PIECE, N), [VMEM] * 4, "join")(recv, halves, mine, top)
    recv = near(lax.all_to_all(send, "y", 0, 0))
    return call(descend_kernel, jax.ShapeDtypeStruct((ROWS, N), F32), [VMEM] * 9, "descend")(
        recv, near(sums), rows, blocks, link, gain, inverses, base, top
    )


def solution(mesh):
    split = Mesh(mesh.devices.reshape(N_OUTER, N_Z, N_Y), ("outer", "z", "y"))
    every = ("outer", "z", "y")
    return jax.shard_map(
        on_device,
        mesh=split,
        in_specs=(
            P(every, None),
            P(every, None),
            P(every, None),
            P(None, every, None),
            P(None, every, None),
            P(),
        ),
        out_specs=P(every, None),
        check_vma=False,
    )
```

```python
import jax
import jax.numpy as jnp
from jax import lax
from jax.experimental import pallas as pl
from jax.experimental.pallas import tpu as pltpu
from jax.sharding import Mesh, PartitionSpec as P

N = 128
BLOCK = 32
PIECE = 16
ROWS = 256
LEVELS = 5
N_Y = 8
N_Z = 16
N_OUTER = 8

F32 = jnp.float32
BF16 = jnp.bfloat16


def split3(value):
    high = value.astype(BF16)
    rest = value - high.astype(F32)
    middle = rest.astype(BF16)
    low = (rest - middle.astype(F32)).astype(BF16)
    return high, middle, low


def dot(left, right, dims):
    return lax.dot_general(left, right, (dims, ((), ())), preferred_element_type=F32)


NN = ((1,), (0,))
NT = ((1,), (1,))


def mm_parts(left, right, dims=NN):
    lh, lm, ll = left
    rh, rm, rl = right
    rows = lh.shape[0]
    first = dot(jnp.concatenate([lh, lm, ll], axis=0), rh, dims)
    second = dot(jnp.concatenate([lh, lm], axis=0), rm, dims)
    third = dot(lh, rl, dims)
    small = first[2 * rows :] + second[rows:] + third
    return first[:rows] + (first[rows : 2 * rows] + second[:rows] + small)


def mm(left, right, dims=NN):
    return mm_parts(split3(left), split3(right), dims)


def mm_exact(left, right, dims=NN):
    rows = left.shape[0]
    lh, lm, ll = split3(left)
    full = dot(jnp.concatenate([lh, lm, ll], axis=0), right, dims)
    return full[:rows] + (full[rows : 2 * rows] + full[2 * rows :])


def iotas(rows=N):
    return (
        lax.broadcasted_iota(jnp.int32, (rows, N), 0),
        lax.broadcasted_iota(jnp.int32, (rows, N), 1),
    )


def mirror_lower(matrix):
    row, col = iotas()
    return jnp.where(row >= col, matrix, matrix.T)


def tri_inverse(triangle):
    row, col = iotas()
    on_diag = row == col
    diag_col = jnp.sum(jnp.where(on_diag, triangle, 0.0), axis=1, keepdims=True)
    diag_row = jnp.sum(jnp.where(on_diag, triangle, 0.0), axis=0, keepdims=True)
    same = (row // BLOCK) == (col // BLOCK)
    strict = jnp.where(same & (row < col), -triangle, 0.0) / diag_col

    same_half = jnp.where(same, 1.0, 0.0).astype(BF16) > 0
    pair_half = jnp.where(row // 64 == col // 64, 1.0, 0.0).astype(BF16) > 0
    zero = jnp.zeros((N, N), BF16)

    def packed(matrix):
        return (matrix[0:32] + matrix[32:64]) + (matrix[64:96] + matrix[96:128])

    def spread(parts, mask, copies):
        return [jnp.where(mask, jnp.concatenate([part] * copies, axis=0), zero) for part in parts]

    def stacked(parts, others):
        return [jnp.concatenate([part, other], axis=0) for part, other in zip(parts, others)]

    small_row, small_col = iotas(BLOCK)
    eye = jnp.where(small_row == small_col % BLOCK, 1.0, 0.0).astype(F32)
    power = packed(strict)
    product = eye + power
    parts = split3(power)
    power = mm_parts(parts, spread(parts, same_half, 4))
    for _ in range(3):
        parts = split3(power)
        both = mm_parts(stacked(parts, split3(product)), spread(parts, same_half, 4))
        product = product + both[BLOCK:]
        power = both[:BLOCK]
    parts = split3(power)
    product = product + mm_parts(split3(product), spread(parts, same_half, 4))
    inverse = product / diag_row
    parts = split3(inverse)
    corner = jnp.where((row // 64 == col // 64) & (row // 32 < col // 32), triangle, 0.0)
    linked = mm_parts(split3(mm_parts(parts, split3(corner))), spread(parts, same_half, 4))
    odd = (small_col // BLOCK) % 2 == 1
    top = jnp.where(odd, -linked, inverse)
    bottom = jnp.where(odd, inverse, 0.0)
    pair = jnp.concatenate([top, bottom], axis=0)
    pair_inverse = jnp.where(row // 64 == col // 64, jnp.concatenate([pair, pair], axis=0), 0.0)
    parts = split3(pair)
    corner = jnp.where(row // 64 < col // 64, triangle, 0.0)
    linked = mm_parts(split3(mm_parts(parts, split3(corner))), spread(parts, pair_half, 2))
    upper = pair_inverse[:64] - linked
    return jnp.concatenate([upper, pair_inverse[64:]], axis=0)


def leaf_kernel(q_hbm, g_hbm, blocks_hbm, sums_ref, send_ref, q_ref, g_ref, blocks_ref, sems):
    copies = [
        pltpu.make_async_copy(g_hbm, g_ref, sems.at[0]),
        pltpu.make_async_copy(q_hbm, q_ref, sems.at[1]),
        pltpu.make_async_copy(blocks_hbm.at[0:2], blocks_ref, sems.at[2]),
    ]
    for copy in copies:
        copy.start()
    copies[0].wait()
    copies[1].wait()
    sums_t = mm(g_ref[...].T, q_ref[...])
    sums_ref[...] = sums_t
    copies[2].wait()
    first_t = mm_exact(sums_t, blocks_ref[0])
    second_t = mm_exact(first_t, blocks_ref[1])
    for y in range(N_Y):
        send_ref[y, 0:PIECE] = first_t[y * PIECE : (y + 1) * PIECE]
        send_ref[y, PIECE : 2 * PIECE] = second_t[y * PIECE : (y + 1) * PIECE]


def near_kernel(z_ref, recv_ref, blocks_ref, after_ref, kept_ref, send_ref):
    z = z_ref[0]
    halves = [sum(recv_ref[4 * h + k, 0:PIECE] for k in range(4)) for h in range(2)]
    kept_ref[0] = halves[0]
    kept_ref[1] = halves[1]
    second = sum(recv_ref[k, PIECE : 2 * PIECE] for k in range(N_Y))
    third = mm_exact(second, blocks_ref[2])
    fourth = mm_exact(third, blocks_ref[3])
    for peer in range(N_Z):
        same_pair = (z // 2) == (peer // 2)
        same_octet = (z // 8) == (peer // 8)
        send_ref[peer] = jnp.where(same_pair, second, jnp.where(same_octet, third, fourth))


def far_kernel(z_ref, recv_ref, blocks_ref, after_ref, kept_ref, send_ref):
    z = z_ref[0]
    zero = jnp.zeros((PIECE, N), F32)
    second, third, fourth = zero, zero, zero
    for peer in range(N_Z):
        same_pair = (z // 2) == (peer // 2)
        same_octet = (z // 8) == (peer // 8)
        value = recv_ref[peer]
        second = second + jnp.where(same_pair, value, zero)
        third = third + jnp.where(same_octet & jnp.logical_not(same_pair), value, zero)
        fourth = fourth + jnp.where(same_octet, zero, value)
    third = third + mm_exact(second, blocks_ref[2])
    fourth = fourth + mm_exact(third, blocks_ref[3])
    fifth = mm_exact(fourth, blocks_ref[4])
    kept_ref[0] = second
    kept_ref[1] = third
    kept_ref[2] = fourth
    for peer in range(N_OUTER):
        send_ref[peer] = fifth


def join_kernel(recv_ref, halves_ref, kept_ref, send_ref):
    fifth = sum(recv_ref[k] for k in range(N_OUTER))
    for y in range(N_Y):
        send_ref[y, 0:PIECE] = halves_ref[y // 4]
        for level in range(3):
            send_ref[y, (level + 1) * PIECE : (level + 2) * PIECE] = kept_ref[level]
        send_ref[y, 4 * PIECE : 5 * PIECE] = fifth


def low_inverse_kernel(tri_ref, tris_ref, after_ref, out_ref):
    out_ref[0] = tri_inverse(tri_ref[...])
    for level in range(2):
        out_ref[level + 1] = tri_inverse(tris_ref[level].astype(F32))


def high_inverse_kernel(tris_ref, after_ref, out_ref):
    for level in range(3):
        out_ref[level] = tri_inverse(tris_ref[level + 2].astype(F32))


def chain_kernel(tri_ref, g_ref, blocks_ref, tris_ref, root_ref, low_ref, high_ref, link_ref, gain_ref, base_ref, top_ref):
    tris = [tri_ref[...]] + [tris_ref[level].astype(F32) for level in range(LEVELS)]
    paths = [None] * (LEVELS + 1)
    paths[LEVELS - 1] = blocks_ref[LEVELS - 1].astype(F32)
    for level in reversed(range(LEVELS - 1)):
        paths[level] = mm(blocks_ref[level].astype(F32), paths[level + 1])
    for level in reversed(range(LEVELS)):
        link = mm(tris[level], low_ref[level + 1] if level < 2 else high_ref[level - 2])
        link_ref[level] = link
        if level == LEVELS - 1:
            gain_ref[level] = link - paths[level]
        else:
            gain_ref[level] = mm(link, paths[level + 1]) - paths[level]
    base_ref[...] = mm(g_ref[...], mm(low_ref[0], paths[0]), NT)
    top_ref[...] = mm(tris[LEVELS], root_ref[...], NT)


def gathered(recv_ref, slot):
    pieces = [recv_ref[y, slot * PIECE : (slot + 1) * PIECE] for y in range(N_Y)]
    return jnp.concatenate(pieces, axis=0)


def descend_kernel(recv_ref, sums_ref, q_ref, blocks_ref, link_ref, gain_ref, low_ref, base_ref, top_ref, out_ref):
    middle = top_ref[...] - gathered(recv_ref, LEVELS - 1)
    for level in reversed(range(LEVELS)):
        own = gathered(recv_ref, level - 1) if level else sums_ref[...]
        spread = mm(link_ref[level], mirror_lower(middle))
        middle = mm(gain_ref[level], own) + mm_exact(spread, blocks_ref[level], NT)
    inner = mm(q_ref[...], mirror_lower(middle))
    out_ref[...] = base_ref[...] + mm(inner, low_ref[0], NT)


def kept(*shape):
    return pltpu.VMEM(shape, F32)


def near(value):
    return pltpu.with_memory_space_constraint(value, pltpu.VMEM)


def far_away(value):
    return pltpu.with_memory_space_constraint(value, pltpu.HBM)


SMEM = pl.BlockSpec(memory_space=pltpu.SMEM)
VMEM = pl.BlockSpec(memory_space=pltpu.VMEM)
PLAIN = pl.BlockSpec(memory_space=pltpu.HBM)


def call(kernel, outs, specs, name, scratch=()):
    return pl.pallas_call(
        kernel,
        in_specs=specs,
        out_shape=outs,
        out_specs=jax.tree.map(lambda _: VMEM, outs),
        scratch_shapes=scratch,
        name=name,
        compiler_params=pltpu.CompilerParams(vmem_limit_bytes=16 << 20),
    )


def on_device(leaf_q, q_cot, leaf_tri, node_blocks, node_tri, root_cot):
    z = lax.axis_index("z").astype(jnp.int32).reshape(1)
    scratch = (
        kept(ROWS, N),
        kept(ROWS, N),
        pltpu.VMEM((2, N, N), BF16),
        pltpu.SemaphoreType.DMA((3,)),
    )
    sums, send = call(
        leaf_kernel, (kept(N, N), kept(N_Y, 2 * PIECE, N)), [PLAIN] * 3, "leaf", scratch
    )(far_away(leaf_q), far_away(q_cot), far_away(node_blocks))
    sums = near(sums)
    blocks, tris = near(node_blocks), near(node_tri)
    tri, cot, root, rows = near(leaf_tri), near(q_cot), near(root_cot), near(leaf_q)

    recv = near(lax.all_to_all(send, "y", 0, 0))
    low = near(call(low_inverse_kernel, kept(3, N, N), [VMEM] * 3, "low")(tri, tris, sums))
    halves, send = call(
        near_kernel, (kept(2, PIECE, N), kept(N_Z, PIECE, N)), [SMEM] + [VMEM] * 3, "near"
    )(z, recv, blocks, low)
    halves = near(halves)

    recv = near(lax.all_to_all(send, "z", 0, 0))
    high = near(call(high_inverse_kernel, kept(3, N, N), [VMEM] * 2, "high")(tris, halves))
    link, gain, base, top = call(
        chain_kernel, (kept(LEVELS, N, N), kept(LEVELS, N, N), kept(ROWS, N), kept(N, N)), [VMEM] * 7, "chain"
    )(tri, cot, blocks, tris, root, low, high)
    link, gain, base, top = near(link), near(gain), near(base), near(top)
    mine, send = call(
        far_kernel, (kept(3, PIECE, N), kept(N_OUTER, PIECE, N)), [SMEM] + [VMEM] * 3, "far"
    )(z, recv, blocks, top)
    mine = near(mine)

    recv = near(lax.all_to_all(send, "outer", 0, 0))
    send = call(join_kernel, kept(N_Y, 5 * PIECE, N), [VMEM] * 3, "join")(recv, halves, mine)

    recv = near(lax.all_to_all(send, "y", 0, 0))
    return call(descend_kernel, jax.ShapeDtypeStruct((ROWS, N), F32), [VMEM] * 9, "descend")(
        recv, sums, rows, blocks, link, gain, low, base, top
    )


def solution(mesh):
    split = Mesh(mesh.devices.reshape(N_OUTER, N_Z, N_Y), ("outer", "z", "y"))
    every = ("outer", "z", "y")
    return jax.shard_map(
        on_device,
        mesh=split,
        in_specs=(
            P(every, None),
            P(every, None),
            P(every, None),
            P(None, every, None),
            P(None, every, None),
            P(),
        ),
        out_specs=P(every, None),
        check_vma=False,
    )
```

```python
import jax
import jax.numpy as jnp
from jax import lax
from jax.experimental import pallas as pl
from jax.experimental.pallas import tpu as pltpu
from jax.sharding import Mesh, PartitionSpec as P

N = 128
BLOCK = 32
PIECE = 16
ROWS = 256
LEVELS = 5
N_Y = 8
N_Z = 16
N_OUTER = 8

F32 = jnp.float32
BF16 = jnp.bfloat16


def split3(value):
    high = value.astype(BF16)
    rest = value - high.astype(F32)
    middle = rest.astype(BF16)
    low = (rest - middle.astype(F32)).astype(BF16)
    return high, middle, low


def dot(left, right, dims):
    return lax.dot_general(left, right, (dims, ((), ())), preferred_element_type=F32)


NN = ((1,), (0,))
NT = ((1,), (1,))


def mm_parts(left, right, dims=NN):
    lh, lm, ll = left
    rh, rm, rl = right
    rows = lh.shape[0]
    first = dot(jnp.concatenate([lh, lm, ll], axis=0), rh, dims)
    second = dot(jnp.concatenate([lh, lm], axis=0), rm, dims)
    third = dot(lh, rl, dims)
    small = first[2 * rows :] + second[rows:] + third
    return first[:rows] + (first[rows : 2 * rows] + second[:rows] + small)


def mm(left, right, dims=NN):
    return mm_parts(split3(left), split3(right), dims)


def mm_exact(left, right, dims=NN):
    rows = left.shape[0]
    lh, lm, ll = split3(left)
    full = dot(jnp.concatenate([lh, lm, ll], axis=0), right, dims)
    return full[:rows] + (full[rows : 2 * rows] + full[2 * rows :])


def split2(value):
    high = value.astype(BF16)
    return high, (value - high.astype(F32)).astype(BF16)


def mm_short(left, right, dims=NN):
    lh, ll = split2(left)
    rh, rl = split2(right)
    wide = jnp.concatenate([lh, ll, lh], axis=1)
    return dot(wide, jnp.concatenate([rh, rh, rl], axis=dims[1][0]), dims)


def mm_exact_short(left, right, dims=NN):
    lh, ll = split2(left)
    wide = jnp.concatenate([ll, lh], axis=1)
    return dot(wide, jnp.concatenate([right, right], axis=dims[1][0]), dims)


def iotas(rows=N):
    return (
        lax.broadcasted_iota(jnp.int32, (rows, N), 0),
        lax.broadcasted_iota(jnp.int32, (rows, N), 1),
    )


def mirror_lower(matrix):
    row, col = iotas()
    return jnp.where(row >= col, matrix, matrix.T)


def tri_inverses(triangles):
    row, col = iotas()
    on_diag = row == col
    same = row // BLOCK == col // BLOCK
    same_pair = row // (2 * BLOCK) == col // (2 * BLOCK)
    same_mask = jnp.where(same, 1.0, 0.0).astype(BF16) > 0
    pair_mask = jnp.where(same_pair, 1.0, 0.0).astype(BF16) > 0
    zero = jnp.zeros((N, N), BF16)
    small_row, small_col = iotas(BLOCK)
    eye = jnp.where(small_row == small_col % BLOCK, 1.0, 0.0).astype(F32)
    odd = (small_col // BLOCK) % 2 == 1

    def packed(matrix):
        return (matrix[0:32] + matrix[32:64]) + (matrix[64:96] + matrix[96:128])

    def spread(parts, mask, copies):
        return [jnp.where(mask, jnp.concatenate([part] * copies, axis=0), zero) for part in parts]

    def stacked(parts, others):
        return [jnp.concatenate(pair, axis=0) for pair in zip(parts, others)]

    def linked(parts, corners, mask, copies):
        left = [mm_parts(part, split3(corner)) for part, corner in zip(parts, corners)]
        return [mm_parts(split3(value), spread(part, mask, copies)) for value, part in zip(left, parts)]

    diags = [jnp.where(on_diag, tri, 0.0) for tri in triangles]
    diag_cols = [jnp.sum(diag, axis=1, keepdims=True) for diag in diags]
    diag_rows = [jnp.sum(diag, axis=0, keepdims=True) for diag in diags]
    powers = [
        packed(jnp.where(same & (row < col), -tri, 0.0) / diag) for tri, diag in zip(triangles, diag_cols)
    ]
    products = [eye + power for power in powers]
    parts = [split3(power) for power in powers]
    powers = [mm_parts(part, spread(part, same_mask, 4)) for part in parts]
    for _ in range(3):
        parts = [split3(power) for power in powers]
        both = [
            mm_parts(stacked(part, split3(product)), spread(part, same_mask, 4))
            for part, product in zip(parts, products)
        ]
        products = [product + value[BLOCK:] for product, value in zip(products, both)]
        powers = [value[:BLOCK] for value in both]
    parts = [split3(power) for power in powers]
    products = [
        product + mm_parts(split3(product), spread(part, same_mask, 4))
        for product, part in zip(products, parts)
    ]
    inverses = [product / diag for product, diag in zip(products, diag_rows)]

    corners = [jnp.where(same_pair & (row // BLOCK < col // BLOCK), tri, 0.0) for tri in triangles]
    links = linked([split3(inverse) for inverse in inverses], corners, same_mask, 4)
    pairs = [
        jnp.concatenate([jnp.where(odd, -link, inverse), jnp.where(odd, inverse, 0.0)], axis=0)
        for link, inverse in zip(links, inverses)
    ]
    corners = [jnp.where(row // (2 * BLOCK) < col // (2 * BLOCK), tri, 0.0) for tri in triangles]
    links = linked([split3(pair) for pair in pairs], corners, pair_mask, 2)
    wide = [jnp.where(same_pair, jnp.concatenate([pair, pair], axis=0), 0.0) for pair in pairs]
    return [jnp.concatenate([full[:64] - link, full[64:]], axis=0) for full, link in zip(wide, links)]


def leaf_kernel(after_ref, q_hbm, g_hbm, blocks_hbm, sums_ref, send_ref, q_ref, g_ref, blocks_ref, sems):
    copies = [
        pltpu.make_async_copy(g_hbm, g_ref, sems.at[0]),
        pltpu.make_async_copy(q_hbm, q_ref, sems.at[1]),
        pltpu.make_async_copy(blocks_hbm.at[0:2], blocks_ref, sems.at[2]),
    ]
    for copy in copies:
        copy.start()
    copies[0].wait()
    copies[1].wait()
    sums_t = mm(g_ref[...].T, q_ref[...])
    sums_ref[...] = sums_t
    copies[2].wait()
    first_t = mm_exact(sums_t, blocks_ref[0])
    second_t = mm_exact(first_t, blocks_ref[1])
    for y in range(N_Y):
        send_ref[y, 0:PIECE] = first_t[y * PIECE : (y + 1) * PIECE]
        send_ref[y, PIECE : 2 * PIECE] = second_t[y * PIECE : (y + 1) * PIECE]


def near_kernel(z_ref, recv_ref, blocks_ref, kept_ref, send_ref):
    z = z_ref[0]
    halves = [sum(recv_ref[4 * h + k, 0:PIECE] for k in range(4)) for h in range(2)]
    kept_ref[0] = halves[0]
    kept_ref[1] = halves[1]
    second = sum(recv_ref[k, PIECE : 2 * PIECE] for k in range(N_Y))
    third = mm_exact(second, blocks_ref[2])
    fourth = mm_exact(third, blocks_ref[3])
    for peer in range(N_Z):
        same_pair = (z // 2) == (peer // 2)
        same_octet = (z // 8) == (peer // 8)
        send_ref[peer] = jnp.where(same_pair, second, jnp.where(same_octet, third, fourth))


def far_kernel(z_ref, recv_ref, blocks_ref, after_ref, kept_ref, send_ref):
    z = z_ref[0]
    zero = jnp.zeros((PIECE, N), F32)
    second, third, fourth = zero, zero, zero
    for peer in range(N_Z):
        same_pair = (z // 2) == (peer // 2)
        same_octet = (z // 8) == (peer // 8)
        value = recv_ref[peer]
        second = second + jnp.where(same_pair, value, zero)
        third = third + jnp.where(same_octet & jnp.logical_not(same_pair), value, zero)
        fourth = fourth + jnp.where(same_octet, zero, value)
    third = third + mm_exact(second, blocks_ref[2])
    fourth = fourth + mm_exact(third, blocks_ref[3])
    fifth = mm_exact(fourth, blocks_ref[4])
    kept_ref[0] = second
    kept_ref[1] = third
    kept_ref[2] = fourth
    for peer in range(N_OUTER):
        send_ref[peer] = fifth


def join_kernel(recv_ref, halves_ref, kept_ref, send_ref):
    fifth = sum(recv_ref[k] for k in range(N_OUTER))
    for y in range(N_Y):
        send_ref[y, 0:PIECE] = halves_ref[y // 4]
        for level in range(3):
            send_ref[y, (level + 1) * PIECE : (level + 2) * PIECE] = kept_ref[level]
        send_ref[y, 4 * PIECE : 5 * PIECE] = fifth


def inverse_kernel(tri_ref, tris_ref, after_ref, out_ref):
    tris = [tri_ref[...]] + [tris_ref[level].astype(F32) for level in range(LEVELS)]
    for level, inverse in enumerate(tri_inverses(tris)):
        out_ref[level] = inverse


def chain_kernel(tri_ref, g_ref, blocks_ref, tris_ref, root_ref, inverse_ref, link_ref, gain_ref, base_ref, top_ref):
    tris = [tri_ref[...]] + [tris_ref[level].astype(F32) for level in range(LEVELS)]
    paths = [None] * (LEVELS + 1)
    paths[LEVELS - 1] = blocks_ref[LEVELS - 1].astype(F32)
    for level in reversed(range(LEVELS - 1)):
        paths[level] = mm(blocks_ref[level].astype(F32), paths[level + 1])
    for level in reversed(range(LEVELS)):
        link = mm(tris[level], inverse_ref[level + 1])
        link_ref[level] = link
        if level == LEVELS - 1:
            gain_ref[level] = link - paths[level]
        else:
            gain_ref[level] = mm(link, paths[level + 1]) - paths[level]
    base_ref[...] = mm(g_ref[...], mm(inverse_ref[0], paths[0]), NT)
    top_ref[...] = mm(tris[LEVELS], root_ref[...], NT)


def gathered(recv_ref, slot):
    pieces = [recv_ref[y, slot * PIECE : (slot + 1) * PIECE] for y in range(N_Y)]
    return jnp.concatenate(pieces, axis=0)


def descend_kernel(
    recv_ref, sums_ref, q_ref, blocks_ref, link_ref, gain_ref, inverse_ref, base_ref, top_ref, out_ref
):
    middle = top_ref[...] - gathered(recv_ref, LEVELS - 1)
    for level in reversed(range(LEVELS)):
        own = gathered(recv_ref, level - 1) if level else sums_ref[...]
        spread = mm_short(link_ref[level], mirror_lower(middle))
        middle = mm_short(gain_ref[level], own) + mm_exact_short(spread, blocks_ref[level], NT)
    last = mm_short(mirror_lower(middle), inverse_ref[0], NT)
    out_ref[...] = base_ref[...] + mm_short(q_ref[...], last)


def kept(*shape):
    return pltpu.VMEM(shape, F32)


def near(value):
    return pltpu.with_memory_space_constraint(value, pltpu.VMEM)


def far_away(value):
    return pltpu.with_memory_space_constraint(value, pltpu.HBM)


SMEM = pl.BlockSpec(memory_space=pltpu.SMEM)
VMEM = pl.BlockSpec(memory_space=pltpu.VMEM)
PLAIN = pl.BlockSpec(memory_space=pltpu.HBM)


def call(kernel, outs, specs, name, scratch=()):
    return pl.pallas_call(
        kernel,
        in_specs=specs,
        out_shape=outs,
        out_specs=jax.tree.map(lambda _: VMEM, outs),
        scratch_shapes=scratch,
        name=name,
        compiler_params=pltpu.CompilerParams(vmem_limit_bytes=16 << 20),
    )


def on_device(leaf_q, q_cot, leaf_tri, node_blocks, node_tri, root_cot):
    z = lax.axis_index("z").astype(jnp.int32).reshape(1)
    scratch = (
        kept(ROWS, N),
        kept(ROWS, N),
        pltpu.VMEM((2, N, N), BF16),
        pltpu.SemaphoreType.DMA((3,)),
    )
    sums, send = call(
        leaf_kernel, (kept(N, N), kept(N_Y, 2 * PIECE, N)), [SMEM] + [PLAIN] * 3, "leaf", scratch
    )(z, far_away(leaf_q), far_away(q_cot), far_away(node_blocks))
    sums = near(sums)
    blocks, tris = near(node_blocks), near(node_tri)
    tri, cot, root, rows = near(leaf_tri), near(q_cot), near(root_cot), near(leaf_q)

    recv = near(lax.all_to_all(send, "y", 0, 0))
    halves, send = call(
        near_kernel, (kept(2, PIECE, N), kept(N_Z, PIECE, N)), [SMEM] + [VMEM] * 2, "near"
    )(z, recv, blocks)
    halves = near(halves)

    recv = near(lax.all_to_all(send, "z", 0, 0))
    inverses = near(call(inverse_kernel, kept(LEVELS + 1, N, N), [VMEM] * 3, "inverse")(tri, tris, halves))
    link, gain, base, top = call(
        chain_kernel, (kept(LEVELS, N, N), kept(LEVELS, N, N), kept(ROWS, N), kept(N, N)), [VMEM] * 6, "chain"
    )(tri, cot, blocks, tris, root, inverses)
    link, gain, base, top = near(link), near(gain), near(base), near(top)
    mine, send = call(
        far_kernel, (kept(3, PIECE, N), kept(N_OUTER, PIECE, N)), [SMEM] + [VMEM] * 3, "far"
    )(z, recv, blocks, top)
    mine = near(mine)

    recv = near(lax.all_to_all(send, "outer", 0, 0))
    send = call(join_kernel, kept(N_Y, 5 * PIECE, N), [VMEM] * 3, "join")(recv, halves, mine)

    recv = near(lax.all_to_all(send, "y", 0, 0))
    return call(descend_kernel, jax.ShapeDtypeStruct((ROWS, N), F32), [VMEM] * 9, "descend")(
        recv, sums, rows, blocks, link, gain, inverses, base, top
    )


def solution(mesh):
    split = Mesh(mesh.devices.reshape(N_OUTER, N_Z, N_Y), ("outer", "z", "y"))
    every = ("outer", "z", "y")
    return jax.shard_map(
        on_device,
        mesh=split,
        in_specs=(
            P(every, None),
            P(every, None),
            P(every, None),
            P(None, every, None),
            P(None, every, None),
            P(),
        ),
        out_specs=P(every, None),
        check_vma=False,
    )
```

```python
import jax
import jax.numpy as jnp
from jax import lax
from jax.experimental import pallas as pl
from jax.experimental.pallas import tpu as pltpu
from jax.sharding import Mesh, PartitionSpec as P

N = 128
BLOCK = 32
PIECE = 8
ROWS = 256
LEVELS = 5
N_NEAR = 16
N_FAR = 8
N_OUTER = 8

F32 = jnp.float32
BF16 = jnp.bfloat16


def split3(value):
    high = value.astype(BF16)
    rest = value - high.astype(F32)
    middle = rest.astype(BF16)
    low = (rest - middle.astype(F32)).astype(BF16)
    return high, middle, low


def dot(left, right, dims):
    return lax.dot_general(left, right, (dims, ((), ())), preferred_element_type=F32)


NN = ((1,), (0,))
NT = ((1,), (1,))


def mm_parts(left, right, dims=NN):
    lh, lm, ll = left
    rh, rm, rl = right
    rows = lh.shape[0]
    first = dot(jnp.concatenate([lh, lm, ll], axis=0), rh, dims)
    second = dot(jnp.concatenate([lh, lm], axis=0), rm, dims)
    third = dot(lh, rl, dims)
    small = first[2 * rows :] + second[rows:] + third
    return first[:rows] + (first[rows : 2 * rows] + second[:rows] + small)


def mm(left, right, dims=NN):
    return mm_parts(split3(left), split3(right), dims)


def mm_exact(left, right, dims=NN):
    rows = left.shape[0]
    lh, lm, ll = split3(left)
    full = dot(jnp.concatenate([lh, lm, ll], axis=0), right, dims)
    return full[:rows] + (full[rows : 2 * rows] + full[2 * rows :])


def split2(value):
    high = value.astype(BF16)
    return high, (value - high.astype(F32)).astype(BF16)


def mm_short(left, right, dims=NN):
    lh, ll = split2(left)
    rh, rl = split2(right)
    wide = jnp.concatenate([lh, ll, lh], axis=1)
    return dot(wide, jnp.concatenate([rh, rh, rl], axis=dims[1][0]), dims)


def mm_exact_short(left, right, dims=NN):
    lh, ll = split2(left)
    wide = jnp.concatenate([ll, lh], axis=1)
    return dot(wide, jnp.concatenate([right, right], axis=dims[1][0]), dims)


def iotas(rows=N):
    return (
        lax.broadcasted_iota(jnp.int32, (rows, N), 0),
        lax.broadcasted_iota(jnp.int32, (rows, N), 1),
    )


def mirror_lower(matrix):
    row, col = iotas()
    return jnp.where(row >= col, matrix, matrix.T)


def tri_inverses(triangles):
    row, col = iotas()
    on_diag = row == col
    same = row // BLOCK == col // BLOCK
    same_pair = row // (2 * BLOCK) == col // (2 * BLOCK)
    same_mask = jnp.where(same, 1.0, 0.0).astype(BF16) > 0
    pair_mask = jnp.where(same_pair, 1.0, 0.0).astype(BF16) > 0
    zero = jnp.zeros((N, N), BF16)
    small_row, small_col = iotas(BLOCK)
    eye = jnp.where(small_row == small_col % BLOCK, 1.0, 0.0).astype(F32)
    odd = (small_col // BLOCK) % 2 == 1

    def packed(matrix):
        return (matrix[0:32] + matrix[32:64]) + (matrix[64:96] + matrix[96:128])

    def spread(parts, mask, copies):
        return [jnp.where(mask, jnp.concatenate([part] * copies, axis=0), zero) for part in parts]

    def stacked(parts, others):
        return [jnp.concatenate(pair, axis=0) for pair in zip(parts, others)]

    def linked(parts, corners, mask, copies):
        left = [mm_parts(part, split3(corner)) for part, corner in zip(parts, corners)]
        return [mm_parts(split3(value), spread(part, mask, copies)) for value, part in zip(left, parts)]

    diags = [jnp.where(on_diag, tri, 0.0) for tri in triangles]
    diag_cols = [jnp.sum(diag, axis=1, keepdims=True) for diag in diags]
    diag_rows = [jnp.sum(diag, axis=0, keepdims=True) for diag in diags]
    powers = [
        packed(jnp.where(same & (row < col), -tri, 0.0) / diag) for tri, diag in zip(triangles, diag_cols)
    ]
    products = [eye + power for power in powers]
    parts = [split3(power) for power in powers]
    powers = [mm_parts(part, spread(part, same_mask, 4)) for part in parts]
    for _ in range(3):
        parts = [split3(power) for power in powers]
        both = [
            mm_parts(stacked(part, split3(product)), spread(part, same_mask, 4))
            for part, product in zip(parts, products)
        ]
        products = [product + value[BLOCK:] for product, value in zip(products, both)]
        powers = [value[:BLOCK] for value in both]
    parts = [split3(power) for power in powers]
    products = [
        product + mm_parts(split3(product), spread(part, same_mask, 4))
        for product, part in zip(products, parts)
    ]
    inverses = [product / diag for product, diag in zip(products, diag_rows)]

    corners = [jnp.where(same_pair & (row // BLOCK < col // BLOCK), tri, 0.0) for tri in triangles]
    links = linked([split3(inverse) for inverse in inverses], corners, same_mask, 4)
    pairs = [
        jnp.concatenate([jnp.where(odd, -link, inverse), jnp.where(odd, inverse, 0.0)], axis=0)
        for link, inverse in zip(links, inverses)
    ]
    corners = [jnp.where(row // (2 * BLOCK) < col // (2 * BLOCK), tri, 0.0) for tri in triangles]
    links = linked([split3(pair) for pair in pairs], corners, pair_mask, 2)
    wide = [jnp.where(same_pair, jnp.concatenate([pair, pair], axis=0), 0.0) for pair in pairs]
    return [jnp.concatenate([full[:64] - link, full[64:]], axis=0) for full, link in zip(wide, links)]


def leaf_kernel(after_ref, q_hbm, g_hbm, blocks_hbm, sums_ref, send_ref, q_ref, g_ref, blocks_ref, sems):
    copies = [
        pltpu.make_async_copy(g_hbm, g_ref, sems.at[0]),
        pltpu.make_async_copy(q_hbm, q_ref, sems.at[1]),
        pltpu.make_async_copy(blocks_hbm.at[0:2], blocks_ref, sems.at[2]),
    ]
    for copy in copies:
        copy.start()
    copies[0].wait()
    copies[1].wait()
    sums_t = mm(g_ref[...].T, q_ref[...])
    sums_ref[...] = sums_t
    copies[2].wait()
    first_t = mm_exact(sums_t, blocks_ref[0])
    second_t = mm_exact(first_t, blocks_ref[1])
    for peer in range(N_NEAR):
        send_ref[peer, 0:PIECE] = first_t[peer * PIECE : (peer + 1) * PIECE]
        send_ref[peer, PIECE : 2 * PIECE] = second_t[peer * PIECE : (peer + 1) * PIECE]


def near_kernel(place_ref, recv_ref, blocks_ref, kept_ref, send_ref):
    place = place_ref[0]
    for group in range(4):
        kept_ref[group] = sum(recv_ref[4 * group + k, 0:PIECE] for k in range(4))
    second = sum(recv_ref[k, PIECE : 2 * PIECE] for k in range(N_NEAR))
    kept_ref[4] = second
    third = mm_exact(second, blocks_ref[2])
    fourth = mm_exact(third, blocks_ref[3])
    for peer in range(N_FAR):
        send_ref[peer] = jnp.where(place // 4 == peer // 4, third, fourth)


def far_kernel(place_ref, recv_ref, blocks_ref, after_ref, kept_ref, send_ref):
    place = place_ref[0]
    zero = jnp.zeros((PIECE, N), F32)
    third, fourth = zero, zero
    for peer in range(N_FAR):
        same = place // 4 == peer // 4
        value = recv_ref[peer]
        third = third + jnp.where(same, value, zero)
        fourth = fourth + jnp.where(same, zero, value)
    fourth = fourth + mm_exact(third, blocks_ref[3])
    fifth = mm_exact(fourth, blocks_ref[4])
    kept_ref[0] = third
    kept_ref[1] = fourth
    for peer in range(N_OUTER):
        send_ref[peer] = fifth


def join_kernel(recv_ref, sums_ref, kept_ref, send_ref):
    fifth = sum(recv_ref[k] for k in range(N_OUTER))
    for peer in range(N_NEAR):
        send_ref[peer, 0:PIECE] = sums_ref[peer // 4]
        send_ref[peer, PIECE : 2 * PIECE] = sums_ref[4]
        send_ref[peer, 2 * PIECE : 3 * PIECE] = kept_ref[0]
        send_ref[peer, 3 * PIECE : 4 * PIECE] = kept_ref[1]
        send_ref[peer, 4 * PIECE : 5 * PIECE] = fifth


def inverse_kernel(tri_ref, tris_ref, after_ref, out_ref):
    tris = [tri_ref[...]] + [tris_ref[level].astype(F32) for level in range(LEVELS)]
    for level, inverse in enumerate(tri_inverses(tris)):
        out_ref[level] = inverse


def chain_kernel(tri_ref, g_ref, blocks_ref, tris_ref, root_ref, inverse_ref, link_ref, gain_ref, base_ref, top_ref):
    tris = [tri_ref[...]] + [tris_ref[level].astype(F32) for level in range(LEVELS)]
    paths = [None] * (LEVELS + 1)
    paths[LEVELS - 1] = blocks_ref[LEVELS - 1].astype(F32)
    for level in reversed(range(LEVELS - 1)):
        paths[level] = mm(blocks_ref[level].astype(F32), paths[level + 1])
    for level in reversed(range(LEVELS)):
        link = mm(tris[level], inverse_ref[level + 1])
        link_ref[level] = link
        if level == LEVELS - 1:
            gain_ref[level] = link - paths[level]
        else:
            gain_ref[level] = mm(link, paths[level + 1]) - paths[level]
    base_ref[...] = mm(g_ref[...], mm(inverse_ref[0], paths[0]), NT)
    top_ref[...] = mm(tris[LEVELS], root_ref[...], NT)


def gathered(recv_ref, slot):
    pieces = [recv_ref[peer, slot * PIECE : (slot + 1) * PIECE] for peer in range(N_NEAR)]
    return jnp.concatenate(pieces, axis=0)


def descend_kernel(
    recv_ref, sums_ref, q_ref, blocks_ref, link_ref, gain_ref, inverse_ref, base_ref, top_ref, out_ref
):
    middle = top_ref[...] - gathered(recv_ref, LEVELS - 1)
    for level in reversed(range(LEVELS)):
        own = gathered(recv_ref, level - 1) if level else sums_ref[...]
        spread = mm_short(link_ref[level], mirror_lower(middle))
        middle = mm_short(gain_ref[level], own) + mm_exact_short(spread, blocks_ref[level], NT)
    last = mm_short(mirror_lower(middle), inverse_ref[0], NT)
    out_ref[...] = base_ref[...] + mm_short(q_ref[...], last)


def kept(*shape):
    return pltpu.VMEM(shape, F32)


def near(value):
    return pltpu.with_memory_space_constraint(value, pltpu.VMEM)


def far_away(value):
    return pltpu.with_memory_space_constraint(value, pltpu.HBM)


SMEM = pl.BlockSpec(memory_space=pltpu.SMEM)
VMEM = pl.BlockSpec(memory_space=pltpu.VMEM)
PLAIN = pl.BlockSpec(memory_space=pltpu.HBM)


def call(kernel, outs, specs, name, scratch=()):
    return pl.pallas_call(
        kernel,
        in_specs=specs,
        out_shape=outs,
        out_specs=jax.tree.map(lambda _: VMEM, outs),
        scratch_shapes=scratch,
        name=name,
        compiler_params=pltpu.CompilerParams(vmem_limit_bytes=16 << 20),
    )


def on_device(leaf_q, q_cot, leaf_tri, node_blocks, node_tri, root_cot):
    place = lax.axis_index("far").astype(jnp.int32).reshape(1)
    scratch = (
        kept(ROWS, N),
        kept(ROWS, N),
        pltpu.VMEM((2, N, N), BF16),
        pltpu.SemaphoreType.DMA((3,)),
    )
    sums, send = call(
        leaf_kernel, (kept(N, N), kept(N_NEAR, 2 * PIECE, N)), [SMEM] + [PLAIN] * 3, "leaf", scratch
    )(place, far_away(leaf_q), far_away(q_cot), far_away(node_blocks))
    sums = near(sums)
    blocks, tris = near(node_blocks), near(node_tri)
    tri, cot, root, rows = near(leaf_tri), near(q_cot), near(root_cot), near(leaf_q)

    recv = near(lax.all_to_all(send, "near", 0, 0))
    low, send = call(
        near_kernel, (kept(5, PIECE, N), kept(N_FAR, PIECE, N)), [SMEM] + [VMEM] * 2, "near"
    )(place, recv, blocks)
    low = near(low)

    recv = near(lax.all_to_all(send, "far", 0, 0))
    inverses = near(call(inverse_kernel, kept(LEVELS + 1, N, N), [VMEM] * 3, "inverse")(tri, tris, low))
    link, gain, base, top = call(
        chain_kernel, (kept(LEVELS, N, N), kept(LEVELS, N, N), kept(ROWS, N), kept(N, N)), [VMEM] * 6, "chain"
    )(tri, cot, blocks, tris, root, inverses)
    link, gain, base, top = near(link), near(gain), near(base), near(top)
    high, send = call(
        far_kernel, (kept(2, PIECE, N), kept(N_OUTER, PIECE, N)), [SMEM] + [VMEM] * 3, "far"
    )(place, recv, blocks, top)
    high = near(high)

    recv = near(lax.all_to_all(send, "outer", 0, 0))
    send = call(join_kernel, kept(N_NEAR, 5 * PIECE, N), [VMEM] * 3, "join")(recv, low, high)

    recv = near(lax.all_to_all(send, "near", 0, 0))
    return call(descend_kernel, jax.ShapeDtypeStruct((ROWS, N), F32), [VMEM] * 9, "descend")(
        recv, sums, rows, blocks, link, gain, inverses, base, top
    )


def solution(mesh):
    every = ("outer", "far", "near")
    split = Mesh(mesh.devices.reshape(N_OUTER, N_FAR, N_NEAR), every)
    return jax.shard_map(
        on_device,
        mesh=split,
        in_specs=(
            P(every, None),
            P(every, None),
            P(every, None),
            P(None, every, None),
            P(None, every, None),
            P(),
        ),
        out_specs=P(every, None),
        check_vma=False,
    )
```

```python
import jax
import jax.numpy as jnp
from jax import lax
from jax.experimental import pallas as pl
from jax.experimental.pallas import tpu as pltpu
from jax.sharding import Mesh, PartitionSpec as P

N = 128
BLOCK = 32
PIECE = 8
ROWS = 256
LEVELS = 5
N_NEAR = 16
N_FAR = 8
N_OUTER = 8

F32 = jnp.float32
BF16 = jnp.bfloat16


def split3(value):
    high = value.astype(BF16)
    rest = value - high.astype(F32)
    middle = rest.astype(BF16)
    low = (rest - middle.astype(F32)).astype(BF16)
    return high, middle, low


def dot(left, right, dims):
    return lax.dot_general(left, right, (dims, ((), ())), preferred_element_type=F32)


NN = ((1,), (0,))
NT = ((1,), (1,))


def mm_parts(left, right, dims=NN):
    lh, lm, ll = left
    rh, rm, rl = right
    rows = lh.shape[0]
    first = dot(jnp.concatenate([lh, lm, ll], axis=0), rh, dims)
    second = dot(jnp.concatenate([lh, lm], axis=0), rm, dims)
    third = dot(lh, rl, dims)
    small = first[2 * rows :] + second[rows:] + third
    return first[:rows] + (first[rows : 2 * rows] + second[:rows] + small)


def mm(left, right, dims=NN):
    return mm_parts(split3(left), split3(right), dims)


def mm_exact_parts(left, right, dims=NN):
    rows = left[0].shape[0]
    full = dot(jnp.concatenate(left, axis=0), right, dims)
    return full[:rows] + (full[rows : 2 * rows] + full[2 * rows :])


def mm_exact(left, right, dims=NN):
    return mm_exact_parts(split3(left), right, dims)


def mm_exact_left(left, right, dims=NN):
    free = 1 - dims[1][0]
    full = dot(left, jnp.concatenate(split3(right), axis=free), dims)
    return full[:, :N] + (full[:, N : 2 * N] + full[:, 2 * N :])


def split2(value):
    high = value.astype(BF16)
    return high, (value - high.astype(F32)).astype(BF16)


def mm_short(left, right, dims=NN):
    lh, ll = split2(left)
    rh, rl = split2(right)
    wide = jnp.concatenate([lh, ll, lh], axis=1)
    return dot(wide, jnp.concatenate([rh, rh, rl], axis=dims[1][0]), dims)


def mm_exact_short(left, right, dims=NN):
    lh, ll = split2(left)
    wide = jnp.concatenate([ll, lh], axis=1)
    return dot(wide, jnp.concatenate([right, right], axis=dims[1][0]), dims)


def iotas(rows=N):
    return (
        lax.broadcasted_iota(jnp.int32, (rows, N), 0),
        lax.broadcasted_iota(jnp.int32, (rows, N), 1),
    )


def mirror_lower(matrix):
    row, col = iotas()
    return jnp.where(row >= col, matrix, matrix.T)


def tri_inverses(triangles):
    row, col = iotas()
    on_diag = row == col
    same = row // BLOCK == col // BLOCK
    same_pair = row // (2 * BLOCK) == col // (2 * BLOCK)
    same_mask = jnp.where(same, 1.0, 0.0).astype(BF16) > 0
    pair_mask = jnp.where(same_pair, 1.0, 0.0).astype(BF16) > 0
    zero = jnp.zeros((N, N), BF16)
    small_row, small_col = iotas(BLOCK)
    eye = jnp.where(small_row == small_col % BLOCK, 1.0, 0.0).astype(F32)
    odd = (small_col // BLOCK) % 2 == 1

    def packed(matrix):
        return (matrix[0:32] + matrix[32:64]) + (matrix[64:96] + matrix[96:128])

    def spread(parts, mask, copies):
        return [jnp.where(mask, jnp.concatenate([part] * copies, axis=0), zero) for part in parts]

    def stacked(parts, others):
        return [jnp.concatenate(pair, axis=0) for pair in zip(parts, others)]

    def linked(parts, corners, mask, copies):
        left = [mm_parts(part, split3(corner)) for part, corner in zip(parts[:1], corners[:1])]
        left += [
            mm_exact_parts(part, corner.astype(BF16)) for part, corner in zip(parts[1:], corners[1:])
        ]
        return [mm_parts(split3(value), spread(part, mask, copies)) for value, part in zip(left, parts)]

    diags = [jnp.where(on_diag, tri, 0.0) for tri in triangles]
    diag_cols = [jnp.sum(diag, axis=1, keepdims=True) for diag in diags]
    diag_rows = [jnp.sum(diag, axis=0, keepdims=True) for diag in diags]
    powers = [
        packed(jnp.where(same & (row < col), -tri, 0.0) / diag) for tri, diag in zip(triangles, diag_cols)
    ]
    products = [eye + power for power in powers]
    parts = [split3(power) for power in powers]
    powers = [mm_parts(part, spread(part, same_mask, 4)) for part in parts]
    for _ in range(3):
        parts = [split3(power) for power in powers]
        both = [
            mm_parts(stacked(part, split3(product)), spread(part, same_mask, 4))
            for part, product in zip(parts, products)
        ]
        products = [product + value[BLOCK:] for product, value in zip(products, both)]
        powers = [value[:BLOCK] for value in both]
    parts = [split3(power) for power in powers]
    products = [
        product + mm_parts(split3(product), spread(part, same_mask, 4))
        for product, part in zip(products, parts)
    ]
    inverses = [product / diag for product, diag in zip(products, diag_rows)]

    corners = [jnp.where(same_pair & (row // BLOCK < col // BLOCK), tri, 0.0) for tri in triangles]
    links = linked([split3(inverse) for inverse in inverses], corners, same_mask, 4)
    pairs = [
        jnp.concatenate([jnp.where(odd, -link, inverse), jnp.where(odd, inverse, 0.0)], axis=0)
        for link, inverse in zip(links, inverses)
    ]
    corners = [jnp.where(row // (2 * BLOCK) < col // (2 * BLOCK), tri, 0.0) for tri in triangles]
    links = linked([split3(pair) for pair in pairs], corners, pair_mask, 2)
    wide = [jnp.where(same_pair, jnp.concatenate([pair, pair], axis=0), 0.0) for pair in pairs]
    return [jnp.concatenate([full[:64] - link, full[64:]], axis=0) for full, link in zip(wide, links)]


def leaf_kernel(after_ref, q_hbm, g_hbm, blocks_hbm, sums_ref, send_ref, q_ref, g_ref, blocks_ref, sems):
    copies = [
        pltpu.make_async_copy(g_hbm, g_ref, sems.at[0]),
        pltpu.make_async_copy(q_hbm, q_ref, sems.at[1]),
        pltpu.make_async_copy(blocks_hbm.at[0:2], blocks_ref, sems.at[2]),
    ]
    for copy in copies:
        copy.start()
    copies[0].wait()
    copies[1].wait()
    sums_t = mm(g_ref[...].T, q_ref[...])
    sums_ref[...] = sums_t
    copies[2].wait()
    first_t = mm_exact(sums_t, blocks_ref[0])
    second_t = mm_exact(first_t, blocks_ref[1])
    for peer in range(N_NEAR):
        send_ref[peer, 0:PIECE] = first_t[peer * PIECE : (peer + 1) * PIECE]
        send_ref[peer, PIECE : 2 * PIECE] = second_t[peer * PIECE : (peer + 1) * PIECE]


def near_kernel(place_ref, recv_ref, blocks_ref, kept_ref, send_ref):
    place = place_ref[0]
    for group in range(4):
        kept_ref[group] = sum(recv_ref[4 * group + k, 0:PIECE] for k in range(4))
    second = sum(recv_ref[k, PIECE : 2 * PIECE] for k in range(N_NEAR))
    kept_ref[4] = second
    third = mm_exact(second, blocks_ref[2])
    fourth = mm_exact(third, blocks_ref[3])
    for peer in range(N_FAR):
        send_ref[peer] = jnp.where(place // 4 == peer // 4, third, fourth)


def far_kernel(place_ref, recv_ref, blocks_ref, after_ref, kept_ref, send_ref):
    place = place_ref[0]
    zero = jnp.zeros((PIECE, N), F32)
    third, fourth = zero, zero
    for peer in range(N_FAR):
        same = place // 4 == peer // 4
        value = recv_ref[peer]
        third = third + jnp.where(same, value, zero)
        fourth = fourth + jnp.where(same, zero, value)
    fourth = fourth + mm_exact(third, blocks_ref[3])
    fifth = mm_exact(fourth, blocks_ref[4])
    kept_ref[0] = third
    kept_ref[1] = fourth
    for peer in range(N_OUTER):
        send_ref[peer] = fifth


def join_kernel(recv_ref, sums_ref, kept_ref, send_ref):
    fifth = sum(recv_ref[k] for k in range(N_OUTER))
    for peer in range(N_NEAR):
        send_ref[peer, 0:PIECE] = sums_ref[peer // 4]
        send_ref[peer, PIECE : 2 * PIECE] = sums_ref[4]
        send_ref[peer, 2 * PIECE : 3 * PIECE] = kept_ref[0]
        send_ref[peer, 3 * PIECE : 4 * PIECE] = kept_ref[1]
        send_ref[peer, 4 * PIECE : 5 * PIECE] = fifth


def inverse_kernel(tri_ref, tris_ref, after_ref, out_ref):
    tris = [tri_ref[...]] + [tris_ref[level].astype(F32) for level in range(LEVELS)]
    for level, inverse in enumerate(tri_inverses(tris)):
        out_ref[level] = inverse


def chain_kernel(
    tri_ref, g_ref, blocks_ref, tris_ref, root_ref, inverse_ref, link_ref, gain_ref, base_ref, top_ref
):
    paths = [None] * LEVELS
    paths[LEVELS - 1] = blocks_ref[LEVELS - 1].astype(F32)
    for level in reversed(range(LEVELS - 1)):
        paths[level] = mm_exact_left(blocks_ref[level], paths[level + 1])
    for level in reversed(range(LEVELS)):
        if level:
            link = mm_exact_left(tris_ref[level - 1], inverse_ref[level + 1])
        else:
            link = mm(tri_ref[...], inverse_ref[1])
        link_ref[level] = link
        if level == LEVELS - 1:
            gain_ref[level] = link - paths[level]
        else:
            gain_ref[level] = mm(link, paths[level + 1]) - paths[level]
    base_ref[...] = mm(g_ref[...], mm(inverse_ref[0], paths[0]), NT)
    top_ref[...] = mm_exact_left(tris_ref[LEVELS - 1], root_ref[...], NT)


def gathered(recv_ref, slot):
    pieces = [recv_ref[peer, slot * PIECE : (slot + 1) * PIECE] for peer in range(N_NEAR)]
    return jnp.concatenate(pieces, axis=0)


def mm_mirrored(left, lower):
    row, col = iotas()
    lh, ll = split2(left)
    ah, al = split2(jnp.where(row >= col, lower, 0.0))
    bh, bl = split2(jnp.where(row > col, lower, 0.0))
    wide = jnp.concatenate([lh, ll, lh], axis=1)
    direct = dot(wide, jnp.concatenate([ah, ah, al], axis=0), NN)
    return direct + dot(wide, jnp.concatenate([bh, bh, bl], axis=1), NT)


def descend_kernel(
    recv_ref, sums_ref, q_ref, blocks_ref, link_ref, gain_ref, inverse_ref, base_ref, top_ref, out_ref
):
    middle = top_ref[...] - gathered(recv_ref, LEVELS - 1)
    for level in reversed(range(LEVELS)):
        own = gathered(recv_ref, level - 1) if level else sums_ref[...]
        spread = mm_mirrored(link_ref[level], middle)
        middle = mm_short(gain_ref[level], own) + mm_exact_short(spread, blocks_ref[level], NT)
    last = mm_short(mirror_lower(middle), inverse_ref[0], NT)
    out_ref[...] = base_ref[...] + mm_short(q_ref[...], last)


def kept(*shape):
    return pltpu.VMEM(shape, F32)


def near(value):
    return pltpu.with_memory_space_constraint(value, pltpu.VMEM)


def far_away(value):
    return pltpu.with_memory_space_constraint(value, pltpu.HBM)


SMEM = pl.BlockSpec(memory_space=pltpu.SMEM)
VMEM = pl.BlockSpec(memory_space=pltpu.VMEM)
PLAIN = pl.BlockSpec(memory_space=pltpu.HBM)


def call(kernel, outs, specs, name, scratch=()):
    return pl.pallas_call(
        kernel,
        in_specs=specs,
        out_shape=outs,
        out_specs=jax.tree.map(lambda _: VMEM, outs),
        scratch_shapes=scratch,
        name=name,
        compiler_params=pltpu.CompilerParams(vmem_limit_bytes=16 << 20),
    )


def on_device(leaf_q, q_cot, leaf_tri, node_blocks, node_tri, root_cot):
    place = lax.axis_index("far").astype(jnp.int32).reshape(1)
    scratch = (
        kept(ROWS, N),
        kept(ROWS, N),
        pltpu.VMEM((2, N, N), BF16),
        pltpu.SemaphoreType.DMA((3,)),
    )
    sums, send = call(
        leaf_kernel, (kept(N, N), kept(N_NEAR, 2 * PIECE, N)), [SMEM] + [PLAIN] * 3, "leaf", scratch
    )(place, far_away(leaf_q), far_away(q_cot), far_away(node_blocks))
    sums = near(sums)
    blocks, tris = near(node_blocks), near(node_tri)
    tri, cot, root, rows = near(leaf_tri), near(q_cot), near(root_cot), near(leaf_q)

    recv = near(lax.all_to_all(send, "near", 0, 0))
    low, send = call(
        near_kernel, (kept(5, PIECE, N), kept(N_FAR, PIECE, N)), [SMEM] + [VMEM] * 2, "near"
    )(place, recv, blocks)
    low = near(low)

    recv = near(lax.all_to_all(send, "far", 0, 0))
    inverses = near(call(inverse_kernel, kept(LEVELS + 1, N, N), [VMEM] * 3, "inverse")(tri, tris, low))
    link, gain, base, top = call(
        chain_kernel, (kept(LEVELS, N, N), kept(LEVELS, N, N), kept(ROWS, N), kept(N, N)), [VMEM] * 6, "chain"
    )(tri, cot, blocks, tris, root, inverses)
    link, gain, base, top = near(link), near(gain), near(base), near(top)
    high, send = call(
        far_kernel, (kept(2, PIECE, N), kept(N_OUTER, PIECE, N)), [SMEM] + [VMEM] * 3, "far"
    )(place, recv, blocks, top)
    high = near(high)

    recv = near(lax.all_to_all(send, "outer", 0, 0))
    send = call(join_kernel, kept(N_NEAR, 5 * PIECE, N), [VMEM] * 3, "join")(recv, low, high)

    recv = near(lax.all_to_all(send, "near", 0, 0))
    return call(descend_kernel, jax.ShapeDtypeStruct((ROWS, N), F32), [VMEM] * 9, "descend")(
        recv, sums, rows, blocks, link, gain, inverses, base, top
    )


def solution(mesh):
    every = ("outer", "far", "near")
    split = Mesh(mesh.devices.reshape(N_OUTER, N_FAR, N_NEAR), every)
    return jax.shard_map(
        on_device,
        mesh=split,
        in_specs=(
            P(every, None),
            P(every, None),
            P(every, None),
            P(None, every, None),
            P(None, every, None),
            P(),
        ),
        out_specs=P(every, None),
        check_vma=False,
    )
```

```python
import jax
import jax.numpy as jnp
from jax import lax
from jax.experimental import pallas as pl
from jax.experimental.pallas import tpu as pltpu
from jax.sharding import Mesh, PartitionSpec as P

N = 128
BLOCK = 32
PIECE = 8
ROWS = 256
LEVELS = 5
N_NEAR = 16
N_FAR = 8
N_OUTER = 8

F32 = jnp.float32
BF16 = jnp.bfloat16


def split3(value):
    high = value.astype(BF16)
    rest = value - high.astype(F32)
    middle = rest.astype(BF16)
    low = (rest - middle.astype(F32)).astype(BF16)
    return high, middle, low


def dot(left, right, dims):
    return lax.dot_general(left, right, (dims, ((), ())), preferred_element_type=F32)


NN = ((1,), (0,))
NT = ((1,), (1,))


def mm_parts(left, right, dims=NN):
    lh, lm, ll = left
    rh, rm, rl = right
    rows = lh.shape[0]
    first = dot(jnp.concatenate([lh, lm, ll], axis=0), rh, dims)
    second = dot(jnp.concatenate([lh, lm], axis=0), rm, dims)
    third = dot(lh, rl, dims)
    small = first[2 * rows :] + second[rows:] + third
    return first[:rows] + (first[rows : 2 * rows] + second[:rows] + small)


def mm(left, right, dims=NN):
    return mm_parts(split3(left), split3(right), dims)


def mm_exact_parts(left, right, dims=NN):
    rows = left[0].shape[0]
    full = dot(jnp.concatenate(left, axis=0), right, dims)
    return full[:rows] + (full[rows : 2 * rows] + full[2 * rows :])


def mm_exact(left, right, dims=NN):
    return mm_exact_parts(split3(left), right, dims)


def mm_exact_left(left, right, dims=NN):
    free = 1 - dims[1][0]
    full = dot(left, jnp.concatenate(split3(right), axis=free), dims)
    return full[:, :N] + (full[:, N : 2 * N] + full[:, 2 * N :])


def split2(value):
    high = value.astype(BF16)
    return high, (value - high.astype(F32)).astype(BF16)


def mm_short(left, right, dims=NN):
    lh, ll = split2(left)
    rh, rl = split2(right)
    wide = jnp.concatenate([lh, ll, lh], axis=1)
    return dot(wide, jnp.concatenate([rh, rh, rl], axis=dims[1][0]), dims)


def mm_exact_short(left, right, dims=NN):
    lh, ll = split2(left)
    wide = jnp.concatenate([ll, lh], axis=1)
    return dot(wide, jnp.concatenate([right, right], axis=dims[1][0]), dims)


def iotas(rows=N):
    return (
        lax.broadcasted_iota(jnp.int32, (rows, N), 0),
        lax.broadcasted_iota(jnp.int32, (rows, N), 1),
    )


def mirror_lower(matrix):
    row, col = iotas()
    return jnp.where(row >= col, matrix, matrix.T)


def tri_inverses(triangles):
    row, col = iotas()
    on_diag = row == col
    same = row // BLOCK == col // BLOCK
    same_pair = row // (2 * BLOCK) == col // (2 * BLOCK)
    same_mask = jnp.where(same, 1.0, 0.0).astype(BF16) > 0
    pair_mask = jnp.where(same_pair, 1.0, 0.0).astype(BF16) > 0
    zero = jnp.zeros((N, N), BF16)
    small_row, small_col = iotas(BLOCK)
    eye = jnp.where(small_row == small_col % BLOCK, 1.0, 0.0).astype(F32)
    odd = (small_col // BLOCK) % 2 == 1

    def packed(matrix):
        return (matrix[0:32] + matrix[32:64]) + (matrix[64:96] + matrix[96:128])

    def spread(parts, mask, copies):
        return [jnp.where(mask, jnp.concatenate([part] * copies, axis=0), zero) for part in parts]

    def stacked(parts, others):
        return [jnp.concatenate(pair, axis=0) for pair in zip(parts, others)]

    def linked(parts, corners, mask, copies):
        left = [mm_parts(part, split3(corner)) for part, corner in zip(parts[:1], corners[:1])]
        left += [
            mm_exact_parts(part, corner.astype(BF16)) for part, corner in zip(parts[1:], corners[1:])
        ]
        return [mm_parts(split3(value), spread(part, mask, copies)) for value, part in zip(left, parts)]

    diags = [jnp.where(on_diag, tri, 0.0) for tri in triangles]
    diag_cols = [jnp.sum(diag, axis=1, keepdims=True) for diag in diags]
    diag_rows = [jnp.sum(diag, axis=0, keepdims=True) for diag in diags]
    powers = [
        packed(jnp.where(same & (row < col), -tri, 0.0) / diag) for tri, diag in zip(triangles, diag_cols)
    ]
    products = [eye + power for power in powers]
    parts = [split3(power) for power in powers]
    powers = [mm_parts(part, spread(part, same_mask, 4)) for part in parts]
    for _ in range(3):
        parts = [split3(power) for power in powers]
        both = [
            mm_parts(stacked(part, split3(product)), spread(part, same_mask, 4))
            for part, product in zip(parts, products)
        ]
        products = [product + value[BLOCK:] for product, value in zip(products, both)]
        powers = [value[:BLOCK] for value in both]
    parts = [split3(power) for power in powers]
    products = [
        product + mm_parts(split3(product), spread(part, same_mask, 4))
        for product, part in zip(products, parts)
    ]
    inverses = [product / diag for product, diag in zip(products, diag_rows)]

    corners = [jnp.where(same_pair & (row // BLOCK < col // BLOCK), tri, 0.0) for tri in triangles]
    links = linked([split3(inverse) for inverse in inverses], corners, same_mask, 4)
    pairs = [
        jnp.concatenate([jnp.where(odd, -link, inverse), jnp.where(odd, inverse, 0.0)], axis=0)
        for link, inverse in zip(links, inverses)
    ]
    corners = [jnp.where(row // (2 * BLOCK) < col // (2 * BLOCK), tri, 0.0) for tri in triangles]
    links = linked([split3(pair) for pair in pairs], corners, pair_mask, 2)
    wide = [jnp.where(same_pair, jnp.concatenate([pair, pair], axis=0), 0.0) for pair in pairs]
    return [jnp.concatenate([full[:64] - link, full[64:]], axis=0) for full, link in zip(wide, links)]


def leaf_kernel(after_ref, q_hbm, g_hbm, blocks_hbm, sums_ref, send_ref, q_ref, g_ref, blocks_ref, sems):
    copies = [
        pltpu.make_async_copy(g_hbm, g_ref, sems.at[0]),
        pltpu.make_async_copy(q_hbm, q_ref, sems.at[1]),
        pltpu.make_async_copy(blocks_hbm.at[0:2], blocks_ref, sems.at[2]),
    ]
    for copy in copies:
        copy.start()
    copies[0].wait()
    copies[1].wait()
    sums_t = mm(g_ref[...].T, q_ref[...])
    sums_ref[...] = sums_t
    copies[2].wait()
    first_t = mm_exact(sums_t, blocks_ref[0])
    second_t = mm_exact(first_t, blocks_ref[1])
    for peer in range(N_NEAR):
        send_ref[peer, 0:PIECE] = first_t[peer * PIECE : (peer + 1) * PIECE]
        send_ref[peer, PIECE : 2 * PIECE] = second_t[peer * PIECE : (peer + 1) * PIECE]


def near_kernel(place_ref, recv_ref, blocks_ref, kept_ref, send_ref):
    place = place_ref[0]
    for group in range(4):
        kept_ref[group] = sum(recv_ref[4 * group + k, 0:PIECE] for k in range(4))
    second = sum(recv_ref[k, PIECE : 2 * PIECE] for k in range(N_NEAR))
    kept_ref[4] = second
    third = mm_exact(second, blocks_ref[2])
    fourth = mm_exact(third, blocks_ref[3])
    for peer in range(N_FAR):
        send_ref[peer] = jnp.where(place // 4 == peer // 4, third, fourth)


def far_kernel(place_ref, recv_ref, blocks_ref, kept_ref, send_ref):
    place = place_ref[0]
    zero = jnp.zeros((PIECE, N), F32)
    third, fourth = zero, zero
    for peer in range(N_FAR):
        same = place // 4 == peer // 4
        value = recv_ref[peer]
        third = third + jnp.where(same, value, zero)
        fourth = fourth + jnp.where(same, zero, value)
    fourth = fourth + mm_exact(third, blocks_ref[3])
    fifth = mm_exact(fourth, blocks_ref[4])
    kept_ref[0] = third
    kept_ref[1] = fourth
    for peer in range(N_OUTER):
        send_ref[peer] = fifth


def join_kernel(recv_ref, sums_ref, kept_ref, send_ref):
    fifth = sum(recv_ref[k] for k in range(N_OUTER))
    for peer in range(N_NEAR):
        send_ref[peer, 0:PIECE] = sums_ref[peer // 4]
        send_ref[peer, PIECE : 2 * PIECE] = sums_ref[4]
        send_ref[peer, 2 * PIECE : 3 * PIECE] = kept_ref[0]
        send_ref[peer, 3 * PIECE : 4 * PIECE] = kept_ref[1]
        send_ref[peer, 4 * PIECE : 5 * PIECE] = fifth


def inverse_kernel(tri_ref, tris_ref, after_ref, out_ref):
    tris = [tri_ref[...]] + [tris_ref[level].astype(F32) for level in range(LEVELS)]
    for level, inverse in enumerate(tri_inverses(tris)):
        out_ref[level] = inverse


def chain_kernel(
    tri_ref, g_ref, blocks_ref, tris_ref, root_ref, inverse_ref, link_ref, gain_ref, base_ref, top_ref
):
    paths = [None] * LEVELS
    paths[LEVELS - 1] = blocks_ref[LEVELS - 1].astype(F32)
    for level in reversed(range(LEVELS - 1)):
        paths[level] = mm_exact_left(blocks_ref[level], paths[level + 1])
    for level in reversed(range(LEVELS)):
        if level:
            link = mm_exact_left(tris_ref[level - 1], inverse_ref[level + 1])
        else:
            link = mm(tri_ref[...], inverse_ref[1])
        link_ref[level] = link
        if level == LEVELS - 1:
            gain_ref[level] = link - paths[level]
        else:
            gain_ref[level] = mm(link, paths[level + 1]) - paths[level]
    base_ref[...] = mm(g_ref[...], mm(inverse_ref[0], paths[0]), NT)
    top_ref[...] = mm_exact_left(tris_ref[LEVELS - 1], root_ref[...], NT)


def gathered(recv_ref, slot):
    pieces = [recv_ref[peer, slot * PIECE : (slot + 1) * PIECE] for peer in range(N_NEAR)]
    return jnp.concatenate(pieces, axis=0)


def mm_mirrored(left, lower):
    row, col = iotas()
    lh, ll = split2(left)
    ah, al = split2(jnp.where(row >= col, lower, 0.0))
    bh, bl = split2(jnp.where(row > col, lower, 0.0))
    wide = jnp.concatenate([lh, ll, lh], axis=1)
    direct = dot(wide, jnp.concatenate([ah, ah, al], axis=0), NN)
    return direct + dot(wide, jnp.concatenate([bh, bh, bl], axis=1), NT)


def descend_kernel(
    recv_ref, sums_ref, q_ref, blocks_ref, link_ref, gain_ref, inverse_ref, base_ref, top_ref, out_ref
):
    middle = top_ref[...] - gathered(recv_ref, LEVELS - 1)
    for level in reversed(range(LEVELS)):
        own = gathered(recv_ref, level - 1) if level else sums_ref[...]
        spread = mm_mirrored(link_ref[level], middle)
        middle = mm_short(gain_ref[level], own) + mm_exact_short(spread, blocks_ref[level], NT)
    last = mm_short(mirror_lower(middle), inverse_ref[0], NT)
    out_ref[...] = base_ref[...] + mm_short(q_ref[...], last)


def kept(*shape):
    return pltpu.VMEM(shape, F32)


def near(value):
    return pltpu.with_memory_space_constraint(value, pltpu.VMEM)


def far_away(value):
    return pltpu.with_memory_space_constraint(value, pltpu.HBM)


SMEM = pl.BlockSpec(memory_space=pltpu.SMEM)
VMEM = pl.BlockSpec(memory_space=pltpu.VMEM)
PLAIN = pl.BlockSpec(memory_space=pltpu.HBM)


def call(kernel, outs, specs, name, scratch=()):
    return pl.pallas_call(
        kernel,
        in_specs=specs,
        out_shape=outs,
        out_specs=jax.tree.map(lambda _: VMEM, outs),
        scratch_shapes=scratch,
        name=name,
        compiler_params=pltpu.CompilerParams(vmem_limit_bytes=16 << 20),
    )


def on_device(leaf_q, q_cot, leaf_tri, node_blocks, node_tri, root_cot):
    place = lax.axis_index("far").astype(jnp.int32).reshape(1)
    scratch = (
        kept(ROWS, N),
        kept(ROWS, N),
        pltpu.VMEM((2, N, N), BF16),
        pltpu.SemaphoreType.DMA((3,)),
    )
    sums, send = call(
        leaf_kernel, (kept(N, N), kept(N_NEAR, 2 * PIECE, N)), [SMEM] + [PLAIN] * 3, "leaf", scratch
    )(place, far_away(leaf_q), far_away(q_cot), far_away(node_blocks))
    sums = near(sums)
    blocks, tris = near(node_blocks), near(node_tri)
    tri, cot, root, rows = near(leaf_tri), near(q_cot), near(root_cot), near(leaf_q)

    recv = near(lax.all_to_all(send, "near", 0, 0))
    low, send = call(
        near_kernel, (kept(5, PIECE, N), kept(N_FAR, PIECE, N)), [SMEM] + [VMEM] * 2, "near"
    )(place, recv, blocks)
    low = near(low)

    recv = near(lax.all_to_all(send, "far", 0, 0))
    high, send = call(
        far_kernel, (kept(2, PIECE, N), kept(N_OUTER, PIECE, N)), [SMEM] + [VMEM] * 2, "far"
    )(place, recv, blocks)
    high = near(high)

    recv = near(lax.all_to_all(send, "outer", 0, 0))
    send = call(join_kernel, kept(N_NEAR, 5 * PIECE, N), [VMEM] * 3, "join")(recv, low, high)

    recv = near(lax.all_to_all(send, "near", 0, 0))
    inverses = near(call(inverse_kernel, kept(LEVELS + 1, N, N), [VMEM] * 3, "inverse")(tri, tris, high))
    link, gain, base, top = call(
        chain_kernel, (kept(LEVELS, N, N), kept(LEVELS, N, N), kept(ROWS, N), kept(N, N)), [VMEM] * 6, "chain"
    )(tri, cot, blocks, tris, root, inverses)
    link, gain, base, top = near(link), near(gain), near(base), near(top)
    return call(descend_kernel, jax.ShapeDtypeStruct((ROWS, N), F32), [VMEM] * 9, "descend")(
        recv, sums, rows, blocks, link, gain, inverses, base, top
    )


def solution(mesh):
    every = ("outer", "far", "near")
    split = Mesh(mesh.devices.reshape(N_OUTER, N_FAR, N_NEAR), every)
    return jax.shard_map(
        on_device,
        mesh=split,
        in_specs=(
            P(every, None),
            P(every, None),
            P(every, None),
            P(None, every, None),
            P(None, every, None),
            P(),
        ),
        out_specs=P(every, None),
        check_vma=False,
    )
```
